32 devices in a mesh: face: 4 (over z), tile: 8 (over y, x, core).
Axes of the slice: x: 2, y: 2, z: 4, core: 2. Of those that a mesh axis runs over, the one named last changes fastest.
Arguments:
- sensitivity: float32 [8, 4, 512, 1536], P(None, None, ('face', 'tile')), may hold values from -6 to 6
- west_weight: float32 [8, 512, 1536], P(None, ('face', 'tile')), may hold values from 0.02 to 0.45
- east_weight: float32 [8, 512, 1536], P(None, ('face', 'tile')), may hold values from 0.02 to 0.45
- south_weight: float32 [8, 512, 1536], P(None, ('face', 'tile')), may hold values from 0.02 to 0.45
- north_weight: float32 [8, 512, 1536], P(None, ('face', 'tile')), may hold values from 0.02 to 0.45
- mixing_rate: float32 [7, 512, 1536], P(None, ('face', 'tile')), may hold values from 0.1 to 10
- extents: int32 [4, 8], replicated, may hold values from 1 to 16, 96 in all within a row
- rotation: int32 [4, 8], replicated, may hold values from 0 to 1
- regrid_weight: bfloat16 [3072, 256, 128], P(('face', 'tile')), may hold values from -0.375 to 0.375
- owner: int32 [3072, 1], P(('face', 'tile')), may hold values from 0 to 31; in each aligned block of 96 rows (0 to 95, 96 to 191, ...) at most 6 rows name the same one
- inv_slot: int32 [3072], P(('face', 'tile')), may hold values from 0 to 7
Outputs:
- adjoint_start: float32 [8, 4, 512, 1536], P(None, None, ('face', 'tile'))
- emission_grad: float32 [256, 4, 128], P(('face', 'tile'))
The draws below stay inside these ranges and needn't reach their ends.
Inputs may be any that keep to these rules, and one draw needn't show every extreme that they name: The 8 extents of each face sum to 96, and the largest of each face is 16. Of the 96 blocks of one tile at most 6 name the same owner, a bound that some block reaches of them.
All inputs are finite; a program needn't handle non-finite values.
Results may differ from the reference program's by a relative error of at most 0.0029.
Values sent between devices are 32-bit elements; how exact they have to be, the bound alone decides.
A program may use at most 128 MiB of HBM per device.

```python
import math
import jax
import jax.numpy as jnp
import numpy as np
from jax import lax

K = 8
S = 4
TILE_ROWS = 16
CY = 1536
RB = 256
EB = 128
NI = 8
NDEV = 32
FACE_ROWS = 96
NB = 96
CB = 6
N_FACE = 4
N_TILE = 8


def plant(values, own_key, least, high):
    shape = values.shape
    spot = [jax.random.randint(jax.random.fold_in(own_key, axis), (), 0, shape[axis]) for axis in range(len(shape))]
    values = values.at[tuple(spot)].set(least)
    longest = shape.index(max(shape))
    spot[longest] = (spot[longest] + 1) % shape[longest]
    return values.at[tuple(spot)].set(high)


def block_levels(stream_key, extent, shards, smallest, top_value):
    level, own = 1.0, jax.random.fold_in(stream_key, 6)
    for position, shards_of in shards:
        heights = jnp.exp(jax.random.uniform(jax.random.fold_in(own, position), (shards_of,), jnp.float32, smallest / len(shards), top_value / len(shards)))
        level = level * jnp.repeat(heights, extent[position] // shards_of).reshape([-1 if axis == position else 1 for axis in range(len(extent))])
    return level


def length_profile(count, total, most, skew):
    weights = [(1 << 20) // math.isqrt(standing ** skew) + 1 for standing in range(2, count + 1)]
    surplus, given = total - most - (count - 1), [1] * (count - 1)
    while surplus > 0:
        free = [i for i in range(count - 1) if given[i] < most]
        pool, budget = sum([weights[i] for i in free]), surplus
        for i in free:
            extra = min(most - given[i], max(1, budget * weights[i] // pool), surplus)
            given[i] = given[i] + extra
            surplus = surplus - extra
    return np.array([most] + given)


def ragged_sizes(rng, amount, total, bound, lean):
    if amount == 2:
        one = jax.random.randint(rng, (), max(1, total - bound), min(bound, total - 1) + 1)
        return jnp.stack([one, total - one])
    lengths = jnp.asarray(length_profile(amount, total, bound, lean), jnp.int32)
    pairs = (amount - 1) // 2
    source_of, sink = lengths[1:1 + 2 * pairs:2], lengths[2:2 + 2 * pairs:2]
    room = jnp.minimum(source_of - 1, bound - sink)
    passed = jax.random.randint(jax.random.fold_in(rng, 1), (pairs,), 0, 1 << 20) % (room + 1)
    lengths = lengths.at[1:1 + 2 * pairs:2].set(source_of - passed).at[2:2 + 2 * pairs:2].set(sink + passed)
    return lengths[jax.random.permutation(jax.random.fold_in(rng, 2), amount)]


def assign_block(stream_key, own, number, rows, count, top, bound, slope):
    sequence = jax.random.permutation(stream_key, count)
    crowded, ordinary = portions_of(count, rows * top, bound, slope, True), portions_of(count, rows * top, bound, slope, False)
    places = jnp.arange(count)

    def named(sizes, offset_by):
        used = int((sizes > 0).sum())
        fixed = max(1, used // 4)
        moved = fixed + (places - fixed + offset_by * (used - fixed)) % max(1, count - fixed)
        return jnp.zeros((count,), jnp.int32).at[sequence[jnp.where(places < fixed, places, moved)]].set(jnp.asarray(sizes, jnp.int32))

    sizes = jnp.where(number % 4 == 0, named(crowded, number // 4), named(ordinary, number - number // 4 - 1))
    mixed = jax.random.permutation(jax.random.fold_in(own, 3), count)
    source_of, taker = mixed[0:count // 2 * 2:2], mixed[1:count // 2 * 2:2]
    slack = jnp.minimum(sizes[source_of] - 1, bound - sizes[taker]) // 2
    slack = jnp.where((source_of == sequence[0]) | (taker == sequence[0]) | (sizes[taker] == 0), 0, jnp.maximum(slack, 0))
    moved = jax.random.randint(jax.random.fold_in(own, 4), (count // 2,), 0, 1 << 20) % (slack + 1)
    sizes = sizes.at[source_of].add(-moved).at[taker].add(moved)
    members = jnp.searchsorted(jnp.cumsum(sizes), jnp.arange(rows * top), side="right").astype(jnp.int32)
    table = members.reshape(top, rows).T
    table = table[jax.random.permutation(jax.random.fold_in(own, 1), rows)]
    offset_by = jax.random.randint(jax.random.fold_in(own, 2), (rows, 1), 0, top)
    return jnp.take_along_axis(table, (jnp.arange(top)[None, :] + offset_by) % top, axis=1)


def portions_of(number_of, total, limit, lean, full):
    portions = [(1 << 20) // math.isqrt(standing ** lean) + 1 for standing in range(1, number_of + 1)]
    largest = limit if full else min(limit, max(-(-total // number_of), total * portions[0] // sum(portions)))
    least = 1 if total - largest >= number_of - 1 else 0
    counts, rest = [largest] + [least] * (number_of - 1), total - largest - least * (number_of - 1)
    while rest > 0:
        free = [i for i in range(1, number_of) if counts[i] < largest] or [i for i in range(1, number_of) if counts[i] < limit]
        whole, budget = sum([portions[i] for i in free]), rest
        for i in free:
            extra = min(limit - counts[i], max(1, budget * portions[i] // whole), rest)
            counts[i] = counts[i] + extra
            rest = rest - extra
    return np.array(counts)


def scatter_about(key, dims, deviation, limit, cuts=(), kind=jnp.bfloat16):
    values = deviation * jax.random.normal(key, dims, jnp.float32)
    if cuts:
        values = values * block_levels(key, dims, cuts, -0.22, 0.18)
    return jnp.clip(values, -limit, limit).astype(kind)


def setup_inputs(seed: int = 0) -> dict:
    arg_keys = jax.random.split(jax.random.key(seed), 12)
    sensitivity = scatter_about(arg_keys[0], (K, S, NDEV * TILE_ROWS, CY), 1.0, 6.0, ((2, 32),), jnp.float32)
    west_weight = jnp.clip(0.02 + 0.42999999 * jax.random.uniform(arg_keys[1], (K, NDEV * TILE_ROWS, CY), jnp.float32) ** block_levels(arg_keys[1], (K, NDEV * TILE_ROWS, CY), ((1, 32),), -0.2, 0.2), 0.02, 0.45)
    east_weight = jnp.clip(0.02 + 0.42999999 * jax.random.uniform(arg_keys[2], (K, NDEV * TILE_ROWS, CY), jnp.float32) ** block_levels(arg_keys[2], (K, NDEV * TILE_ROWS, CY), ((1, 32),), -0.2, 0.2), 0.02, 0.45)
    south_weight = jnp.clip(0.02 + 0.42999999 * jax.random.uniform(arg_keys[3], (K, NDEV * TILE_ROWS, CY), jnp.float32) ** block_levels(arg_keys[3], (K, NDEV * TILE_ROWS, CY), ((1, 32),), -0.2, 0.2), 0.02, 0.45)
    north_weight = jnp.clip(0.02 + 0.42999999 * jax.random.uniform(arg_keys[4], (K, NDEV * TILE_ROWS, CY), jnp.float32) ** block_levels(arg_keys[4], (K, NDEV * TILE_ROWS, CY), ((1, 32),), -0.2, 0.2), 0.02, 0.45)
    mixing_rate = jnp.clip(jnp.exp(math.log(10.0) - 4.6051702 * jax.random.uniform(arg_keys[5], (K - 1, NDEV * TILE_ROWS, CY), jnp.float32) ** block_levels(arg_keys[5], (K - 1, NDEV * TILE_ROWS, CY), ((1, 32),), -0.2, 0.2)), 0.1, 10.0)
    extents = jax.vmap(lambda own: ragged_sizes(own, N_TILE, FACE_ROWS, TILE_ROWS, 2))(jax.random.split(arg_keys[6], N_FACE)).reshape((N_FACE, N_TILE)).astype(jnp.int32)
    rotation = plant(jax.random.randint(arg_keys[7], (N_FACE, N_TILE), 0, 2), jax.random.fold_in(arg_keys[7], 1), 0, 1).astype(jnp.int32)
    regrid_weight = scatter_about(arg_keys[8], (NDEV * NB, RB, EB), RB ** -0.5, 0.375, ((0, 32),))
    owner_keys = jax.random.split(jax.random.fold_in(arg_keys[9], 1), (NDEV * NB) // NB)
    owner_turns = jax.random.permutation(jax.random.fold_in(arg_keys[9], 3), (NDEV * NB) // NB)
    owner = jax.vmap(lambda own, number: assign_block(jax.random.fold_in(arg_keys[9], 2), own, number, NB, NDEV, 1, CB, 2))(owner_keys, owner_turns).reshape((NDEV * NB, 1))
    inv_slot = plant(jax.random.randint(arg_keys[10], (NDEV * NB,), 0, NI), jax.random.fold_in(arg_keys[10], 1), 0, NI - 1).astype(jnp.int32)
    return {"sensitivity": sensitivity, "west_weight": west_weight, "east_weight": east_weight, "south_weight": south_weight, "north_weight": north_weight, "mixing_rate": mixing_rate, "extents": extents, "rotation": rotation, "regrid_weight": regrid_weight, "owner": owner, "inv_slot": inv_slot}


def meridional(adjoint, south_rate, north_rate):
    south_flux = south_rate * adjoint
    north_flux = north_rate * adjoint
    edge_zero = jnp.zeros_like(adjoint[..., :1])
    return ((1.0 - south_rate - north_rate) * adjoint
            + jnp.concatenate([south_flux[..., 1:], edge_zero], axis=-1)
            + jnp.concatenate([edge_zero, north_flux[..., :-1]], axis=-1))


def vertical_solve(rhs, rate):
    count = rhs.shape[0]
    diagonal_terms = []
    for level in range(count):
        value = 1.0 + jnp.zeros_like(rate[0])
        if level > 0:
            value = value + rate[level - 1]
        if level < count - 1:
            value = value + rate[level]
        diagonal_terms.append(value)
    pivot = diagonal_terms[0]
    upper_part = [-rate[0] / pivot]
    solved = [rhs[0] / pivot]
    for level in range(1, count):
        pivot = diagonal_terms[level] + rate[level - 1] * upper_part[-1]
        if level < count - 1:
            upper_part.append(-rate[level] / pivot)
        solved.append((rhs[level] + rate[level - 1] * solved[-1]) / pivot)
    result = [solved[-1]]
    for level in range(count - 2, -1, -1):
        result.insert(0, solved[level] - upper_part[level] * result[0])
    return jnp.stack(result)


def reference(sensitivity, west_weight, east_weight, south_weight, north_weight, mixing_rate, extents, rotation, regrid_weight, owner, inv_slot):
    device_count = N_FACE * N_TILE
    ext_all = extents.reshape(device_count)
    rot_all = rotation.reshape(device_count)
    row_ids = jnp.arange(TILE_ROWS, dtype=jnp.int32)
    ftype = sensitivity.dtype
    live_rows = (row_ids[None, :] < ext_all[:, None]).astype(ftype)[:, :, None]
    first_pick = (row_ids == 0).astype(ftype)[None, :, None]
    last_pick = (row_ids[None, :] == ext_all[:, None] - 1).astype(ftype)[:, :, None]
    shape_five = (K, 1, device_count, TILE_ROWS, CY)
    adjoint = sensitivity.reshape(K, S, device_count, TILE_ROWS, CY) * live_rows
    west_rate = west_weight.reshape(shape_five)
    east_rate = east_weight.reshape(shape_five)
    west_flux = west_rate * adjoint
    east_flux = east_rate * adjoint
    east_edge = jnp.sum(east_flux * last_pick, axis=3)
    west_edge = west_flux[:, :, :, 0, :]
    from_west = jnp.roll(east_edge, 1, axis=2)
    from_west = jnp.where(rot_all[None, None, :, None] == 1, jnp.flip(from_west, -1), from_west)
    from_east = jnp.roll(west_edge, -1, axis=2)
    rot_next = jnp.roll(rot_all, -1)
    from_east = jnp.where(rot_next[None, None, :, None] == 1, jnp.flip(from_east, -1), from_east)
    zero_row = jnp.zeros_like(adjoint[:, :, :, :1])
    moved = ((1.0 - west_rate - east_rate) * adjoint
             + jnp.concatenate([west_flux[:, :, :, 1:], zero_row], axis=3)
             + jnp.concatenate([zero_row, east_flux[:, :, :, :-1]], axis=3))
    moved = (moved + first_pick * from_west[:, :, :, None] + last_pick * from_east[:, :, :, None]) * live_rows
    moved = meridional(moved, south_weight.reshape(shape_five), north_weight.reshape(shape_five))
    rate = mixing_rate.reshape(K - 1, 1, device_count, TILE_ROWS, CY)
    adjoint_start = vertical_solve(moved, rate)
    surface = adjoint_start[0].astype(jnp.bfloat16)
    surface = jnp.transpose(surface, (1, 0, 2, 3)).reshape(device_count, S, NB, RB)
    weights = regrid_weight.reshape(device_count, NB, RB, EB)

    def one_tile(pair):
        tile_surface, tile_weight = pair
        return jnp.einsum('snr,nre->nse', tile_surface.astype(jnp.float32), tile_weight.astype(jnp.float32), precision=lax.Precision.HIGHEST)

    terms = lax.map(one_tile, (surface, weights))
    target = (owner.reshape(-1) * NI + inv_slot).astype(jnp.int32)
    grad = jax.ops.segment_sum(terms.reshape(device_count * NB, S * EB), target, num_segments=device_count * NI)
    return adjoint_start.reshape(K, S, device_count * TILE_ROWS, CY), grad.reshape(device_count * NI, S, EB)
```

```python
import functools

import jax
import jax.numpy as jnp
from jax import lax
from jax.experimental import pallas as pl
from jax.experimental.pallas import tpu as pltpu
from jax.sharding import PartitionSpec as P

NI = 8
LANES = 128
SUB = 8
MESH = pl.DeviceIdType.MESH
F32 = jnp.float32
BF16 = jnp.bfloat16


def pieces(value, number):
    parts = []
    for _ in range(number):
        part = value.astype(BF16)
        parts.append(part)
        value = value - part.astype(F32)
    return parts


def column(c):
    return slice(c * LANES, (c + 1) * LANES)


def step_kernel(faces, tiles, ext_hbm, rot_hbm, sens_hbm, west_hbm, east_hbm, south_hbm, north_hbm,
                rate_hbm, regrid_hbm, owner_hbm, slot_hbm, solved, grad_ref,
                sens_v, west_v, east_v, south_v, north_v, rate_v, regrid_v, inverse_v, carry_v, upper_v,
                east_edge, west_edge, from_west, from_east, edge_rates, flat, own_terms, their_terms, own_ids, their_ids,
                sums, in_b, sum_c, in_c,
                ext_ref, rot_ref, owner_ref, slot_ref, small_sem, level_sem, rate_sem, regrid_sem,
                east_send, east_recv, west_send, west_recv, ids_sem, send_a, recv_a, send_b, recv_b, send_c, recv_c):
    levels, species, rows, width = sens_v.shape
    chunks = width // LANES
    blocks, cells, inv_cells = regrid_v.shape
    per_row = width // cells
    lane_parts = cells // LANES
    group = SUB // species
    groups = levels // group
    face, tile = lax.axis_index("face"), lax.axis_index("tile")
    count, chips = faces * tiles, tiles // 2
    position = face * tiles + tile
    after, before = lax.rem(position + 1, count), lax.rem(position + count - 1, count)
    after = (after // tiles, lax.rem(after, tiles))
    before = (before // tiles, lax.rem(before, tiles))
    chip, core = tile // 2, lax.rem(tile, 2)
    partner = (face, tile + 1 - 2 * core)
    chip_of = [lax.rem(chip + step, chips) for step in range(chips)]
    face_of = [lax.rem(face + step, faces) for step in range(faces)]
    others = [after, before, partner]
    others += [(face, 2 * chip_of[step] + core) for step in range(1, chips)]
    others += [(face_of[step], tile) for step in range(1, faces)]
    barrier = pltpu.get_barrier_semaphore()
    for other in others:
        pl.semaphore_signal(barrier, inc=1, device_id=other, device_id_type=MESH)

    def level_copies(level, pairs, base):
        return [
            pltpu.make_async_copy(source.at[level], sink.at[level], level_sem.at[base + number, level])
            for number, (source, sink) in enumerate(pairs)
        ]

    x_pairs = ((sens_hbm, sens_v), (west_hbm, west_v), (east_hbm, east_v))
    y_pairs = ((south_hbm, south_v), (north_hbm, north_v))
    rates = pltpu.make_async_copy(rate_hbm, rate_v.at[pl.ds(1, levels - 1)], rate_sem)
    regrid = pltpu.make_async_copy(regrid_hbm, regrid_v, regrid_sem)
    small = [
        pltpu.make_async_copy(source, sink, small_sem.at[number])
        for number, (source, sink) in enumerate(
            ((ext_hbm, ext_ref), (rot_hbm, rot_ref), (owner_hbm, owner_ref), (slot_hbm, slot_ref)))
    ]
    for copy in small:
        copy.start()
    for level in range(levels):
        for copy in level_copies(level, x_pairs, 0):
            copy.start()
    rates.start()
    for level in range(levels):
        for copy in level_copies(level, y_pairs, 3):
            copy.start()
    regrid.start()

    for copy in small:
        copy.wait()
    extent = ext_ref[face, tile]
    row_ids = lax.broadcasted_iota(jnp.int32, (rows, LANES), 0)
    lane_ids = lax.broadcasted_iota(jnp.int32, (rows, LANES), 1)
    live = row_ids < extent
    first, last = row_ids == 0, row_ids == extent - 1
    west_live = jnp.logical_and(live, row_ids > 0)
    east_live = row_ids < extent - 1
    lane_first, lane_last = lane_ids == 0, lane_ids == LANES - 1
    zero = jnp.zeros((rows, LANES), F32)
    zero_field = jnp.zeros((rows, width), F32)
    rate_v[0] = zero_field
    rate_v[levels] = zero_field
    upper_v[0] = zero_field

    half_k = own_ids.shape[1]
    block_of = lax.broadcasted_iota(jnp.int32, (blocks, half_k), 1)
    block_of = jnp.where(block_of < blocks, lax.rem(block_of, rows) * per_row + block_of // rows, -1)
    permute = lax.broadcasted_iota(jnp.int32, (blocks, half_k), 0) == block_of
    permute = permute.astype(F32).astype(BF16)

    def permuted(ref):
        value = jnp.broadcast_to(ref[...].astype(F32), (SUB, blocks)).astype(BF16)
        return jnp.dot(value, permute, preferred_element_type=F32)

    ids = permuted(owner_ref) * float(NI) + permuted(slot_ref)
    own_ids[...] = jnp.where(lax.broadcasted_iota(jnp.int32, (SUB, half_k), 1) < blocks, ids, -1.0)

    after_rotation = rot_ref[after[0], after[1]]
    my_rotation = rot_ref[face, tile]
    back = (lax.broadcasted_iota(jnp.int32, (LANES, LANES), 0)
            + lax.broadcasted_iota(jnp.int32, (LANES, LANES), 1) == LANES - 1)
    back = back.astype(F32).astype(BF16)
    edge_ids = lax.broadcasted_iota(jnp.int32, (SUB, LANES), 0)

    def edge_copies(part):
        return (
            pltpu.make_async_remote_copy(
                src_ref=east_edge.at[part], dst_ref=from_west.at[part],
                send_sem=east_send.at[part], recv_sem=east_recv.at[part],
                device_id=after, device_id_type=MESH),
            pltpu.make_async_remote_copy(
                src_ref=west_edge.at[part], dst_ref=from_east.at[part],
                send_sem=west_send.at[part], recv_sem=west_recv.at[part],
                device_id=before, device_id_type=MESH),
        )

    def turn(values, rotation):
        straight = jnp.concatenate(values, axis=0)
        turned = sum(jnp.dot(piece, back, preferred_element_type=F32) for piece in pieces(straight, 3))
        reverse = jnp.full((SUB, LANES), rotation, jnp.int32) == 1
        return [
            jnp.where(reverse, turned[(chunks - 1 - c) * SUB:(chunks - c) * SUB], values[c])
            for c in range(chunks)
        ]

    pl.semaphore_wait(barrier, len(others))
    send_ids = pltpu.make_async_remote_copy(
        src_ref=own_ids, dst_ref=their_ids, send_sem=ids_sem.at[0], recv_sem=ids_sem.at[1],
        device_id=partner, device_id_type=MESH)
    send_ids.start()

    def edges(part, carry):
        east_values, west_values = [None] * chunks, [None] * chunks
        for j in range(group):
            level = part * group + j
            for copy in level_copies(level, x_pairs, 0):
                copy.wait()
            for c in range(chunks):
                east_rows = jnp.where(last, east_v[level, :, column(c)], 0.0)
                west_row = west_v[level, 0:1, column(c)]
                for kind in range(species):
                    east = jnp.sum(east_rows * sens_v[level, kind, :, column(c)], axis=0, keepdims=True)
                    west = west_row * sens_v[level, kind, 0:1, column(c)]
                    east = jnp.broadcast_to(east, (SUB, LANES))
                    west = jnp.broadcast_to(west, (SUB, LANES))
                    number = j * species + kind
                    if number == 0:
                        east_values[c], west_values[c] = east, west
                    else:
                        here = edge_ids == number
                        east_values[c] = jnp.where(here, east, east_values[c])
                        west_values[c] = jnp.where(here, west, west_values[c])
        east_values = turn(east_values, after_rotation)
        west_values = turn(west_values, my_rotation)
        for c in range(chunks):
            east_edge[part, :, column(c)] = east_values[c]
            west_edge[part, :, column(c)] = west_values[c]
        for copy in edge_copies(part):
            copy.start()
        return carry

    lax.fori_loop(0, groups, edges, 0)

    rates.wait()

    def stencils(level, carry):
        for copy in level_copies(level, y_pairs, 3):
            copy.wait()
        held, behind = None, [zero] * species
        for c in range(chunks + 1):
            fresh = [(None, zero, zero)] * species
            if c < chunks:
                cols = column(c)
                west, east = west_v[level, :, cols], east_v[level, :, cols]
                south, north = south_v[level, :, cols], north_v[level, :, cols]
                keep_x = jnp.where(live, 1.0 - west - east, 0.0)
                west = jnp.where(west_live, west, 0.0)
                east = jnp.where(east_live, east, 0.0)
                keep_y = 1.0 - south - north
                fresh = []
                for kind in range(species):
                    value = sens_v[level, kind, :, cols]
                    moved = (keep_x * value + pltpu.roll(west * value, rows - 1, 0)
                             + pltpu.roll(east * value, 1, 0))
                    fresh.append((
                        keep_y * moved,
                        pltpu.roll(south * moved, LANES - 1, 1),
                        pltpu.roll(north * moved, 1, 1),
                    ))
                low, high = rate_v[level, :, cols], rate_v[level + 1, :, cols]
                inverse = 1.0 / ((1.0 + low + high) + low * upper_v[level, :, cols])
                upper_v[level + 1, :, cols] = -high * inverse
                inverse_v[level, :, cols] = inverse
                carry_v[level, :, cols] = low * inverse
            if c > 0:
                cols = column(c - 1)
                for kind in range(species):
                    centre, left, right = held[kind]
                    solved[level, kind, :, cols] = (
                        centre + jnp.where(lane_last, fresh[kind][1], left)
                        + jnp.where(lane_first, behind[kind], right))
                behind = [held[kind][2] for kind in range(species)]
            held = fresh
        return carry

    lax.fori_loop(0, levels, stencils, 0)

    used = blocks * species
    spare = jnp.zeros((own_terms.shape[0] - used, inv_cells), F32)
    own_terms[used:, :] = spare
    their_terms[used:, :] = spare
    small_first, small_last = lane_first[:SUB], lane_last[:SUB]
    nothing = jnp.zeros((SUB, LANES), F32)

    def edge_weights(part, carry):
        for number, ref in enumerate((south_v, north_v)):
            for c in range(chunks):
                cols = column(c)
                head = tail = None
                for j in range(group):
                    field = ref[part * group + j, :, cols]
                    top = jnp.broadcast_to(field[0:1], (SUB, LANES))
                    end = jnp.broadcast_to(
                        jnp.sum(jnp.where(last, field, 0.0), axis=0, keepdims=True), (SUB, LANES))
                    here = edge_ids >= j * species
                    head = top if j == 0 else jnp.where(here, top, head)
                    tail = end if j == 0 else jnp.where(here, end, tail)
                edge_rates[number, part, :, cols] = head
                edge_rates[2 + number, part, :, cols] = tail
        return carry

    lax.fori_loop(0, groups, edge_weights, 0)

    def edge_stencils(part, carry):
        for copy in edge_copies(part):
            copy.wait_recv()
        for side, ref in enumerate((from_west, from_east)):
            held, behind = None, nothing
            for c in range(chunks + 1):
                fresh = (None, nothing, nothing)
                if c < chunks:
                    cols = column(c)
                    south, north = edge_rates[2 * side, part, :, cols], edge_rates[2 * side + 1, part, :, cols]
                    moved = ref[part, :, cols]
                    fresh = ((1.0 - south - north) * moved,
                             pltpu.roll(south * moved, LANES - 1, 1), pltpu.roll(north * moved, 1, 1))
                if c > 0:
                    centre, left, right = held
                    ref[part, :, column(c - 1)] = (
                        centre + jnp.where(small_last, fresh[1], left) + jnp.where(small_first, behind, right))
                    behind = right
                held = fresh
        return carry

    lax.fori_loop(0, groups, edge_stencils, 0)

    def term_copy(part):
        span = pl.ds(part * rows * species, rows * species)
        return pltpu.make_async_remote_copy(
            src_ref=own_terms.at[span], dst_ref=their_terms.at[span],
            send_sem=send_a.at[part], recv_sem=recv_a.at[part],
            device_id=partner, device_id_type=MESH)

    upper_half = edge_ids < species
    for part in range(per_row):
        for c in range(part * lane_parts, (part + 1) * lane_parts):
            cols = column(c)
            for kind in range(species):
                below, held = None, []
                for level in range(levels):
                    number = level % group * species + kind
                    west = from_west[level // group, number:number + 1, cols]
                    east = from_east[level // group, number:number + 1, cols]
                    value = (solved[level, kind, :, cols] + jnp.where(first, west, 0.0)
                             + jnp.where(last, east, 0.0)) * inverse_v[level, :, cols]
                    if level > 0:
                        value = value + carry_v[level, :, cols] * below
                    below = value
                    held.append(value)
                for level in range(levels - 1, -1, -1):
                    value = held[level]
                    if level < levels - 1:
                        value = value - upper_v[level + 1, :, cols] * below
                    solved[level, kind, :, cols] = value
                    below = value
                flat[c, pl.ds(kind, rows, stride=species), :] = below
        if part == 0:
            regrid.wait()
        for pair in range(rows // group):
            lines = slice(pair * SUB, (pair + 1) * SUB)
            surface = jnp.concatenate(
                [flat[part * lane_parts + p, lines, :] for p in range(lane_parts)], axis=1).astype(BF16)
            weights = jnp.concatenate(
                [regrid_v[(pair * group + j) * per_row + part] for j in range(group)], axis=1)
            product = jnp.dot(surface, weights, preferred_element_type=F32)
            value = product[:, :inv_cells]
            for j in range(1, group):
                value = jnp.where(edge_ids >= j * species, product[:, j * inv_cells:(j + 1) * inv_cells], value)
            own_terms[part * rows * species + pair * SUB:part * rows * species + (pair + 1) * SUB, :] = value
        term_copy(part).start()

    send_ids.wait_recv()
    unit = faces * NI
    height = chips * unit
    place = lax.broadcasted_iota(jnp.int32, (height, half_k), 0)
    to_chip = chip + place // unit
    to_chip = jnp.where(to_chip >= chips, to_chip - chips, to_chip)
    to_face = face + lax.rem(place, unit) // NI
    to_face = jnp.where(to_face >= faces, to_face - faces, to_face)
    target = ((to_face * tiles + 2 * to_chip + core) * NI + lax.rem(place, NI)).astype(F32)
    select = jnp.concatenate(
        [(jnp.broadcast_to(ref[0:1, :], (height, half_k)) == target).astype(F32) for ref in (own_ids, their_ids)],
        axis=1).astype(BF16)
    for part in range(per_row):
        term_copy(part).wait_recv()
    values = jnp.concatenate(
        [jnp.concatenate([ref[pl.ds(kind, half_k, stride=species), :] for kind in range(species)], axis=1)
         for ref in (own_terms, their_terms)], axis=0)
    total = sum(jnp.dot(select, piece, preferred_element_type=F32) for piece in pieces(values, 2))
    for step in range(chips):
        for spot in range(faces):
            start = step * unit + spot * NI
            sums[step, spot] = total[start:start + NI]

    spots = list(range(1, faces)) + [0]
    second, third = {}, {}
    for spot in spots:
        for step in range(1, chips):
            second[step, spot] = pltpu.make_async_remote_copy(
                src_ref=sums.at[step, spot], dst_ref=in_b.at[step - 1, spot],
                send_sem=send_b.at[step - 1, spot], recv_sem=recv_b.at[step - 1, spot],
                device_id=(face, 2 * chip_of[step] + core), device_id_type=MESH)
            second[step, spot].start()
    result = None
    for spot in spots:
        result = sums[0, spot]
        for step in range(1, chips):
            second[step, spot].wait_recv()
            result = result + in_b[step - 1, spot]
        if spot > 0:
            sum_c[spot - 1] = result
            third[spot] = pltpu.make_async_remote_copy(
                src_ref=sum_c.at[spot - 1], dst_ref=in_c.at[spot - 1],
                send_sem=send_c.at[spot - 1], recv_sem=recv_c.at[spot - 1],
                device_id=(face_of[spot], tile), device_id_type=MESH)
            third[spot].start()
    for spot in range(1, faces):
        third[spot].wait_recv()
        result = result + in_c[spot - 1]
    for kind in range(species):
        grad_ref[:, kind, :] = result[:, kind * inv_cells:(kind + 1) * inv_cells]
    send_ids.wait_send()
    for part in range(groups):
        for copy in edge_copies(part):
            copy.wait_send()
    for part in range(per_row):
        term_copy(part).wait_send()
    for copies in (second, third):
        for copy in copies.values():
            copy.wait_send()


def write_kernel(solved, grad, solved_out, grad_out, level_sem, grad_sem):
    copies = [pltpu.make_async_copy(grad, grad_out, grad_sem)]
    copies += [
        pltpu.make_async_copy(solved.at[level], solved_out.at[level], level_sem.at[level])
        for level in range(solved.shape[0])
    ]
    for copy in copies:
        copy.start()
    for copy in copies:
        copy.wait()


def per_device(faces, tiles, sensitivity, west_weight, east_weight, south_weight, north_weight,
               mixing_rate, extents, rotation, regrid_weight, owner, inv_slot):
    levels, species, rows, width = sensitivity.shape
    blocks, cells, inv_cells = regrid_weight.shape
    chips = tiles // 2
    hbm = pl.BlockSpec(memory_space=pltpu.HBM)
    vmem = pl.BlockSpec(memory_space=pltpu.VMEM)
    dma = pltpu.SemaphoreType.DMA
    groups = levels * species // SUB
    half_k = -(-blocks // LANES) * LANES
    field, line = (levels, rows, width), (groups, SUB, width)
    more = (levels + 1, rows, width)
    scratch = [pltpu.VMEM(shape, F32) for shape in [sensitivity.shape] + [field] * 4 + [more]]
    scratch += [pltpu.VMEM(regrid_weight.shape, regrid_weight.dtype)]
    shapes = [field, field, more] + [line] * 4 + [(4,) + line]
    shapes += [(width // LANES, rows * species, LANES)] + [(half_k * species, inv_cells)] * 2
    shapes += [(SUB, half_k)] * 2
    unit = (NI, species * inv_cells)
    shapes += [(chips, faces) + unit, (chips - 1, faces) + unit, (faces - 1,) + unit, (faces - 1,) + unit]
    scratch += [pltpu.VMEM(shape, F32) for shape in shapes]
    scratch += [pltpu.SMEM(extents.shape, jnp.int32)] * 2 + [pltpu.VMEM((1, blocks), jnp.int32)] * 2
    scratch += [dma((4,)), dma((5, levels)), dma, dma]
    scratch += [dma((groups,))] * 4 + [dma((2,))] + [dma((width // cells,))] * 2
    scratch += [dma((chips - 1, faces))] * 2 + [dma((faces - 1,))] * 2
    pin = functools.partial(pltpu.with_memory_space_constraint, memory_space=pltpu.HBM)
    operands = (extents, rotation, sensitivity, west_weight, east_weight, south_weight, north_weight,
                mixing_rate, regrid_weight, owner.reshape(1, blocks), inv_slot.reshape(1, blocks))
    outs = (
        jax.ShapeDtypeStruct(sensitivity.shape, F32),
        jax.ShapeDtypeStruct((NI, species, inv_cells), F32),
    )
    solved, grad = pl.pallas_call(
        functools.partial(step_kernel, faces, tiles),
        out_shape=outs,
        in_specs=[hbm] * 11,
        out_specs=(vmem, vmem),
        scratch_shapes=scratch,
        compiler_params=pltpu.CompilerParams(
            collective_id=0, has_side_effects=True, vmem_limit_bytes=44 << 20),
        name="step",
    )(*[pin(operand) for operand in operands])
    return pl.pallas_call(
        write_kernel,
        out_shape=outs,
        in_specs=[vmem, vmem],
        out_specs=(hbm, hbm),
        scratch_shapes=[dma((levels,)), dma],
        compiler_params=pltpu.CompilerParams(vmem_limit_bytes=8 << 20),
        name="write",
    )(solved, grad)


def solution(mesh):
    faces, tiles = mesh.shape["face"], mesh.shape["tile"]
    both = ("face", "tile")
    placed = (P(None, None, both, None),) + (P(None, both, None),) * 5 + (P(), P()) + (
        P(both, None, None), P(both, None), P(both))
    return jax.shard_map(
        functools.partial(per_device, faces, tiles),
        mesh=mesh,
        in_specs=placed,
        out_specs=(P(None, None, both, None), P(both, None, None)),
        check_vma=False,
    )
```

```python
import functools

import jax
import jax.numpy as jnp
from jax import lax
from jax.experimental import pallas as pl
from jax.experimental.pallas import tpu as pltpu
from jax.sharding import PartitionSpec as P

NI = 8
LANES = 128
SUB = 8
MESH = pl.DeviceIdType.MESH
F32 = jnp.float32
BF16 = jnp.bfloat16


def pieces(value, number):
    parts = []
    for _ in range(number):
        part = value.astype(BF16)
        parts.append(part)
        value = value - part.astype(F32)
    return parts


def column(c):
    return slice(c * LANES, (c + 1) * LANES)


def step_kernel(faces, tiles, ext_hbm, rot_hbm, sens_hbm, west_hbm, east_hbm, south_hbm, north_hbm,
                rate_hbm, regrid_hbm, owner_hbm, slot_hbm, solved, grad_ref,
                sens_v, west_v, east_v, south_v, north_v, rate_v, regrid_v, inverse_v, carry_v, upper_v,
                east_edge, west_edge, from_west, from_east, edge_rates, edge, flat, own_terms, their_terms, own_ids, their_ids,
                sums, in_b, sum_c, in_c,
                ext_ref, rot_ref, owner_ref, slot_ref, small_sem, level_sem, rate_sem, regrid_sem,
                east_send, east_recv, west_send, west_recv, ids_sem, send_a, recv_a, send_b, recv_b, send_c, recv_c):
    levels, species, rows, width = sens_v.shape
    chunks = width // LANES
    _, per_row, cells, inv_cells = regrid_v.shape
    blocks = rows * per_row
    lane_parts = cells // LANES
    group = SUB // species
    groups = levels // group
    ahead = groups - 1
    early = 2 * (groups - 2)
    face, tile = lax.axis_index("face"), lax.axis_index("tile")
    count, chips = faces * tiles, tiles // 2
    position = face * tiles + tile
    after, before = lax.rem(position + 1, count), lax.rem(position + count - 1, count)
    after = (after // tiles, lax.rem(after, tiles))
    before = (before // tiles, lax.rem(before, tiles))
    chip, core = tile // 2, lax.rem(tile, 2)
    partner = (face, tile + 1 - 2 * core)
    chip_of = [lax.rem(chip + step, chips) for step in range(chips)]
    face_of = [face]
    for step in range(1, faces):
        down, up = faces - step, step - 1
        down = down - (down <= face).astype(jnp.int32)
        up = up + (up >= face).astype(jnp.int32)
        face_of.append(jnp.where(face < faces // 2, down, up))
    others = [after, before, partner]
    others += [(face, 2 * chip_of[step] + core) for step in range(1, chips)]
    others += [(face_of[step], tile) for step in range(1, faces)]
    barrier = pltpu.get_barrier_semaphore()
    for other in others:
        pl.semaphore_signal(barrier, inc=1, device_id=other, device_id_type=MESH)

    def level_copies(level, pairs, base):
        return [
            pltpu.make_async_copy(source.at[level], sink.at[level], level_sem.at[base + number, level])
            for number, (source, sink) in enumerate(pairs)
        ]

    x_pairs = ((sens_hbm, sens_v), (west_hbm, west_v), (east_hbm, east_v))
    y_pairs = ((south_hbm, south_v), (north_hbm, north_v))
    rates = pltpu.make_async_copy(rate_hbm, rate_v.at[pl.ds(1, levels - 1)], rate_sem)

    def regrid_copy(part):
        return pltpu.make_async_copy(regrid_hbm.at[:, part], regrid_v.at[:, part], regrid_sem.at[part])

    small = [
        pltpu.make_async_copy(source, sink, small_sem.at[number])
        for number, (source, sink) in enumerate(
            ((ext_hbm, ext_ref), (rot_hbm, rot_ref), (owner_hbm, owner_ref), (slot_hbm, slot_ref)))
    ]
    for copy in small:
        copy.start()

    def start_group(part, pairs, base):
        for j in range(group):
            for copy in level_copies(part * group + j, pairs, base):
                copy.start()

    for part in range(ahead):
        start_group(part, x_pairs, 0)

    for copy in small:
        copy.wait()
    extent = ext_ref[face, tile]
    row_ids = lax.broadcasted_iota(jnp.int32, (rows, LANES), 0)
    lane_ids = lax.broadcasted_iota(jnp.int32, (rows, LANES), 1)
    live = row_ids < extent
    first, last = row_ids == 0, row_ids == extent - 1
    west_live = jnp.logical_and(live, row_ids > 0)
    east_live = row_ids < extent - 1
    lane_first, lane_last = lane_ids == 0, lane_ids == LANES - 1
    zero = jnp.zeros((rows, LANES), F32)
    zero_field = jnp.zeros((rows, width), F32)
    rate_v[0] = zero_field
    rate_v[levels] = zero_field
    upper_v[0] = zero_field

    after_rotation = rot_ref[after[0], after[1]]
    my_rotation = rot_ref[face, tile]
    back = (lax.broadcasted_iota(jnp.int32, (LANES, LANES), 0)
            + lax.broadcasted_iota(jnp.int32, (LANES, LANES), 1) == LANES - 1)
    back = back.astype(F32).astype(BF16)
    edge_ids = lax.broadcasted_iota(jnp.int32, (SUB, LANES), 0)

    final_row = jnp.maximum(extent - 1, 0)
    final_rows = jnp.full((SUB, LANES), final_row, jnp.int32)
    final_low = final_rows < SUB
    to_row = [lax.rem(number + rows - final_row, SUB) for number in range(SUB)]

    def final_half(field):
        return jnp.where(final_low, field[:SUB], field[SUB:])

    def edge_copies(part):
        return (
            pltpu.make_async_remote_copy(
                src_ref=east_edge.at[part], dst_ref=from_west.at[part],
                send_sem=east_send.at[part], recv_sem=east_recv.at[part],
                device_id=after, device_id_type=MESH),
            pltpu.make_async_remote_copy(
                src_ref=west_edge.at[part], dst_ref=from_east.at[part],
                send_sem=west_send.at[part], recv_sem=west_recv.at[part],
                device_id=before, device_id_type=MESH),
        )

    def turn(values, rotation):
        straight = jnp.concatenate(values, axis=0)
        turned = sum(jnp.dot(piece, back, preferred_element_type=F32) for piece in pieces(straight, 3))
        reverse = jnp.full((SUB, LANES), rotation, jnp.int32) == 1
        return [
            jnp.where(reverse, turned[(chunks - 1 - c) * SUB:(chunks - c) * SUB], values[c])
            for c in range(chunks)
        ]

    hold = groups // 2 - 1

    def edges(part, carry):
        east_values, west_values = [None] * chunks, [None] * chunks
        for j in range(group):
            level = part * group + j
            for copy in level_copies(level, x_pairs, 0):
                copy.wait()

        @pl.when(part == 0)
        def _():
            for later in range(ahead, groups):
                start_group(later, x_pairs, 0)
            rates.start()

        @pl.when(part == 1)
        def _():
            for later in range(groups):
                start_group(later, y_pairs, 3)

        @pl.when(part > 1)
        def _():
            for each in range(2):
                regrid_copy(2 * (part - 2) + each).start()

        for j in range(group):
            level = part * group + j
            for c in range(chunks):
                cols = column(c)
                east_half = final_half(east_v[level, :, cols])
                west_half = west_v[level, 0:SUB, cols]
                for kind in range(species):
                    value = sens_v[level, kind, :, cols]
                    east = east_half * final_half(value)
                    west = west_half * value[:SUB]
                    number = j * species + kind
                    east = pltpu.roll(east, to_row[number], 0)
                    if number == 0:
                        east_values[c], west_values[c] = east, west
                    else:
                        here = edge_ids == number
                        east_values[c] = jnp.where(here, east, east_values[c])
                        west_values[c] = jnp.where(here, pltpu.roll(west, number, 0), west_values[c])
        east_values = turn(east_values, after_rotation)
        west_values = turn(west_values, my_rotation)
        for c in range(chunks):
            east_edge[part, :, column(c)] = east_values[c]
            west_edge[part, :, column(c)] = west_values[c]

        @pl.when(part == hold)
        def _():
            pl.semaphore_wait(barrier, len(others))
            for sooner in range(hold):
                for copy in edge_copies(sooner):
                    copy.start()

        @pl.when(part >= hold)
        def _():
            for copy in edge_copies(part):
                copy.start()

        return carry

    lax.fori_loop(0, groups, edges, 0)
    half_k = own_ids.shape[1]
    block_of = lax.broadcasted_iota(jnp.int32, (blocks, half_k), 1)
    spare = block_of - blocks
    edge_row = jnp.where(lax.rem(spare, 2) == 0, 0, extent - 1)
    block_of = jnp.where(block_of < blocks, lax.rem(block_of, rows) * per_row + block_of // rows,
                         edge_row * per_row + spare // 2)
    permute = lax.broadcasted_iota(jnp.int32, (blocks, half_k), 0) == block_of
    permute = permute.astype(F32).astype(BF16)

    def permuted(ref):
        value = jnp.broadcast_to(ref[...].astype(F32), (SUB, blocks)).astype(BF16)
        return jnp.dot(value, permute, preferred_element_type=F32)

    ids = permuted(owner_ref) * float(NI) + permuted(slot_ref)
    spot_ids = lax.broadcasted_iota(jnp.int32, (SUB, half_k), 1)
    row_of, side_of = lax.rem(spot_ids, rows), lax.rem(spot_ids, 2)
    inner = jnp.logical_and(spot_ids < blocks, jnp.logical_and(row_of > 0, row_of != extent - 1))
    outer = jnp.logical_and(jnp.logical_and(spot_ids >= blocks, spot_ids < blocks + 2 * per_row),
                            jnp.logical_or(side_of == 0, extent > 1))
    own_ids[...] = jnp.where(jnp.logical_or(inner, outer), ids, -1.0)

    send_ids = pltpu.make_async_remote_copy(
        src_ref=own_ids, dst_ref=their_ids, send_sem=ids_sem.at[0], recv_sem=ids_sem.at[1],
        device_id=partner, device_id_type=MESH)
    send_ids.start()
    rates.wait()

    upper_half = edge_ids < species

    def edge_rows(field):
        tail = pltpu.roll(final_half(field), to_row[0], 0)
        return jnp.where(upper_half, jnp.broadcast_to(field[0:1], (SUB, LANES)),
                         jnp.broadcast_to(tail[0:1], (SUB, LANES)))

    def stencils(level, carry):
        for copy in level_copies(level, y_pairs, 3):
            copy.wait()

        @pl.when(level + early < per_row)
        def _():
            regrid_copy(level + early).start()

        held, behind = None, [zero] * species
        for c in range(chunks + 1):
            fresh = [(None, zero, zero)] * species
            if c < chunks:
                cols = column(c)
                west, east = west_v[level, :, cols], east_v[level, :, cols]
                south, north = south_v[level, :, cols], north_v[level, :, cols]
                keep_x = jnp.where(live, 1.0 - west - east, 0.0)
                west = jnp.where(west_live, west, 0.0)
                east = jnp.where(east_live, east, 0.0)
                keep_y = 1.0 - south - north
                fresh = []
                for kind in range(species):
                    value = sens_v[level, kind, :, cols]
                    moved = (keep_x * value + pltpu.roll(west * value, rows - 1, 0)
                             + pltpu.roll(east * value, 1, 0))
                    fresh.append((
                        keep_y * moved,
                        pltpu.roll(south * moved, LANES - 1, 1),
                        pltpu.roll(north * moved, 1, 1),
                    ))
                low, high = rate_v[level, :, cols], rate_v[level + 1, :, cols]
                inverse = 1.0 / ((1.0 + low + high) + low * upper_v[level, :, cols])
                upper = -high * inverse
                upper_v[level + 1, :, cols] = upper
                inverse_v[level, :, cols] = inverse
                carry_v[level, :, cols] = low * inverse
                for number, field in enumerate((south, north, inverse, low * inverse, upper)):
                    edge_rates[number, level, :, cols] = edge_rows(field)
            if c > 0:
                cols = column(c - 1)
                for kind in range(species):
                    centre, left, right = held[kind]
                    solved[level, kind, :, cols] = (
                        centre + jnp.where(lane_last, fresh[kind][1], left)
                        + jnp.where(lane_first, behind[kind], right))
                behind = [held[kind][2] for kind in range(species)]
            held = fresh
        return carry

    lax.fori_loop(0, levels, stencils, 0)

    used = (blocks + 2 * per_row) * species
    spare = jnp.zeros((own_terms.shape[0] - used, inv_cells), F32)
    own_terms[used:, :] = spare
    their_terms[used:, :] = spare

    def term_copy(part):
        if part < per_row:
            span = pl.ds(part * rows * species, rows * species)
        else:
            span = pl.ds(blocks * species, per_row * SUB)
        return pltpu.make_async_remote_copy(
            src_ref=own_terms.at[span], dst_ref=their_terms.at[span],
            send_sem=send_a.at[part], recv_sem=recv_a.at[part],
            device_id=partner, device_id_type=MESH)

    def solve(part):
        for c in range(part * lane_parts, (part + 1) * lane_parts):
            cols = column(c)
            for kind in range(species):
                below, held = None, []
                for level in range(levels):
                    value = solved[level, kind, :, cols] * inverse_v[level, :, cols]
                    if level > 0:
                        value = value + carry_v[level, :, cols] * below
                    below = value
                    held.append(value)
                for level in range(levels - 1, -1, -1):
                    value = held[level]
                    if level < levels - 1:
                        value = value - upper_v[level + 1, :, cols] * below
                    solved[level, kind, :, cols] = value
                    below = value
                flat[c, pl.ds(kind, rows, stride=species), :] = below

    def regridded(surface, weights):
        product = jnp.dot(surface.astype(BF16), jnp.concatenate(weights, axis=1), preferred_element_type=F32)
        value = product[:, :inv_cells]
        for j in range(1, len(weights)):
            value = jnp.where(edge_ids >= j * species, product[:, j * inv_cells:(j + 1) * inv_cells], value)
        return value

    solve(0)
    for part in range(per_row):
        regrid_copy(part).wait()
        if part + 1 < per_row:
            solve(part + 1)
        for pair in range(rows // group):
            lines = slice(pair * SUB, (pair + 1) * SUB)
            surface = jnp.concatenate(
                [flat[part * lane_parts + p, lines, :] for p in range(lane_parts)], axis=1)
            weights = [regrid_v[pair * group + j, part] for j in range(group)]
            start = part * rows * species + pair * SUB
            own_terms[start:start + SUB, :] = regridded(surface, weights)
        term_copy(part).start()

    small_first, small_last = lane_first[:SUB], lane_last[:SUB]
    nothing = jnp.zeros((SUB, LANES), F32)

    def edge_forward(part, carry):
        for copy in edge_copies(part):
            copy.wait_recv()
        for j in range(group):
            level = part * group + j
            previous = jnp.maximum(level - 1, 0)
            held, behind = None, nothing
            for c in range(chunks + 1):
                fresh = (None, nothing, nothing)
                if c < chunks:
                    cols = column(c)
                    south, north = edge_rates[0, level, :, cols], edge_rates[1, level, :, cols]
                    west, east = from_west[part, :, cols], from_east[part, :, cols]
                    if j > 0:
                        west = pltpu.roll(west, SUB - j * species, 0)
                    if j < group - 1:
                        east = pltpu.roll(east, SUB - (j + 1) * species, 0)
                    moved = jnp.where(upper_half, west, east)
                    fresh = ((1.0 - south - north) * moved,
                             pltpu.roll(south * moved, LANES - 1, 1), pltpu.roll(north * moved, 1, 1))
                if c > 0:
                    cols = column(c - 1)
                    centre, left, right = held
                    value = centre + jnp.where(small_last, fresh[1], left) + jnp.where(small_first, behind, right)
                    edge[level, :, cols] = (value * edge_rates[2, level, :, cols]
                                            + edge_rates[3, level, :, cols] * edge[previous, :, cols])
                    behind = right
                held = fresh
        return carry

    edge[0] = jnp.zeros((SUB, width), F32)
    lax.fori_loop(0, groups, edge_forward, 0)
    odd = lax.rem(final_rows, group) == 1
    lone = jnp.logical_and(upper_half, final_rows == 0)
    surfaces = []
    for c in range(chunks):
        cols = column(c)
        below = edge[levels - 1, :, cols]
        for level in range(levels - 2, -1, -1):
            below = edge[level, :, cols] - edge_rates[4, level, :, cols] * below
            edge[level, :, cols] = below
        slab = flat[c, 0:SUB, :]
        for pair in range(1, rows // group):
            slab = jnp.where(final_rows >= pair * group, flat[c, pair * SUB:(pair + 1) * SUB, :], slab)
        slab = jnp.where(odd, slab, pltpu.roll(slab, species, 0))
        below = below + jnp.where(lone, pltpu.roll(below, species, 0), 0.0)
        surfaces.append(below + jnp.where(upper_half, flat[c, 0:SUB, :], slab))
    for part in range(per_row):
        surface = jnp.concatenate(surfaces[part * lane_parts:(part + 1) * lane_parts], axis=1)
        start = blocks * species + part * SUB
        own_terms[start:start + SUB, :] = regridded(surface, [regrid_v[0, part], regrid_v[final_row, part]])
    term_copy(per_row).start()

    send_ids.wait_recv()
    unit = faces * NI
    height = chips * unit
    place = lax.broadcasted_iota(jnp.int32, (height, half_k), 0)
    to_chip = chip + place // unit
    to_chip = jnp.where(to_chip >= chips, to_chip - chips, to_chip)
    spot_of = lax.rem(place, unit) // NI
    to_face = jnp.full((height, half_k), face, jnp.int32)
    for spot in range(1, faces):
        to_face = jnp.where(spot_of == spot, face_of[spot], to_face)
    target = ((to_face * tiles + 2 * to_chip + core) * NI + lax.rem(place, NI)).astype(F32)
    select = jnp.concatenate(
        [(jnp.broadcast_to(ref[0:1, :], (height, half_k)) == target).astype(F32) for ref in (own_ids, their_ids)],
        axis=1).astype(BF16)
    for part in range(per_row + 1):
        term_copy(part).wait_recv()
    values = jnp.concatenate(
        [jnp.concatenate([ref[pl.ds(kind, half_k, stride=species), :] for kind in range(species)], axis=1)
         for ref in (own_terms, their_terms)], axis=0)
    total = sum(jnp.dot(select, piece, preferred_element_type=F32) for piece in pieces(values, 2))
    for step in range(chips):
        for spot in range(faces):
            start = step * unit + spot * NI
            sums[step, spot] = total[start:start + NI]

    spots = list(range(1, faces)) + [0]
    second, third = {}, {}
    for spot in spots:
        for step in range(1, chips):
            second[step, spot] = pltpu.make_async_remote_copy(
                src_ref=sums.at[step, spot], dst_ref=in_b.at[step - 1, spot],
                send_sem=send_b.at[step - 1, spot], recv_sem=recv_b.at[step - 1, spot],
                device_id=(face, 2 * chip_of[step] + core), device_id_type=MESH)
            second[step, spot].start()

    def add_edges(level, carry):
        for c in range(chunks):
            cols = column(c)
            for kind in range(species):
                solved[level, kind, :, cols] = (
                    solved[level, kind, :, cols] + jnp.where(first, edge[level, kind:kind + 1, cols], 0.0)
                    + jnp.where(last, edge[level, species + kind:species + kind + 1, cols], 0.0))
        return carry

    lax.fori_loop(0, levels, add_edges, 0)
    result = None
    for spot in spots:
        result = sums[0, spot]
        for step in range(1, chips):
            second[step, spot].wait_recv()
            result = result + in_b[step - 1, spot]
        if spot > 0:
            sum_c[spot - 1] = result
            third[spot] = pltpu.make_async_remote_copy(
                src_ref=sum_c.at[spot - 1], dst_ref=in_c.at[face],
                send_sem=send_c.at[spot - 1], recv_sem=recv_c.at[face],
                device_id=(face_of[spot], tile), device_id_type=MESH)
            third[spot].start()
    for spot in range(1, faces):
        pltpu.make_async_remote_copy(
            src_ref=sum_c.at[spot - 1], dst_ref=in_c.at[face_of[spot]],
            send_sem=send_c.at[spot - 1], recv_sem=recv_c.at[face_of[spot]],
            device_id=(face_of[spot], tile), device_id_type=MESH).wait_recv()
        result = result + in_c[face_of[spot]]
    for kind in range(species):
        grad_ref[:, kind, :] = result[:, kind * inv_cells:(kind + 1) * inv_cells]
    send_ids.wait_send()
    for part in range(groups):
        for copy in edge_copies(part):
            copy.wait_send()
    for part in range(per_row + 1):
        term_copy(part).wait_send()
    for copies in (second, third):
        for copy in copies.values():
            copy.wait_send()


def write_kernel(solved, grad, solved_out, grad_out, level_sem, grad_sem):
    copies = [pltpu.make_async_copy(grad, grad_out, grad_sem)]
    copies += [
        pltpu.make_async_copy(solved.at[level], solved_out.at[level], level_sem.at[level])
        for level in range(solved.shape[0])
    ]
    for copy in copies:
        copy.start()
    for copy in copies:
        copy.wait()


def per_device(faces, tiles, sensitivity, west_weight, east_weight, south_weight, north_weight,
               mixing_rate, extents, rotation, regrid_weight, owner, inv_slot):
    levels, species, rows, width = sensitivity.shape
    blocks, cells, inv_cells = regrid_weight.shape
    chips = tiles // 2
    hbm = pl.BlockSpec(memory_space=pltpu.HBM)
    vmem = pl.BlockSpec(memory_space=pltpu.VMEM)
    dma = pltpu.SemaphoreType.DMA
    groups = levels * species // SUB
    per_row = width // cells
    half_k = -(-(blocks + 2 * per_row) // LANES) * LANES
    field, line = (levels, rows, width), (groups, SUB, width)
    more = (levels + 1, rows, width)
    scratch = [pltpu.VMEM(shape, F32) for shape in [sensitivity.shape] + [field] * 4 + [more]]
    regrid_weight = regrid_weight.reshape(rows, per_row, cells, inv_cells)
    scratch += [pltpu.VMEM(regrid_weight.shape, regrid_weight.dtype)]
    shapes = [field, field, more] + [line] * 4 + [(5, levels, SUB, width), (levels, SUB, width)]
    shapes += [(width // LANES, rows * species, LANES)] + [(half_k * species, inv_cells)] * 2
    shapes += [(SUB, half_k)] * 2
    unit = (NI, species * inv_cells)
    shapes += [(chips, faces) + unit, (chips - 1, faces) + unit, (faces - 1,) + unit, (faces,) + unit]
    scratch += [pltpu.VMEM(shape, F32) for shape in shapes]
    scratch += [pltpu.SMEM(extents.shape, jnp.int32)] * 2 + [pltpu.VMEM((1, blocks), jnp.int32)] * 2
    scratch += [dma((4,)), dma((5, levels)), dma, dma((per_row,))]
    scratch += [dma((groups,))] * 4 + [dma((2,))] + [dma((per_row + 1,))] * 2
    scratch += [dma((chips - 1, faces))] * 2 + [dma((faces - 1,)), dma((faces,))]
    pin = functools.partial(pltpu.with_memory_space_constraint, memory_space=pltpu.HBM)
    operands = (extents, rotation, sensitivity, west_weight, east_weight, south_weight, north_weight,
                mixing_rate, regrid_weight, owner.reshape(1, blocks), inv_slot.reshape(1, blocks))
    outs = (
        jax.ShapeDtypeStruct(sensitivity.shape, F32),
        jax.ShapeDtypeStruct((NI, species, inv_cells), F32),
    )
    solved, grad = pl.pallas_call(
        functools.partial(step_kernel, faces, tiles),
        out_shape=outs,
        in_specs=[hbm] * 11,
        out_specs=(vmem, vmem),
        scratch_shapes=scratch,
        compiler_params=pltpu.CompilerParams(
            collective_id=0, has_side_effects=True, vmem_limit_bytes=44 << 20),
        name="step",
    )(*[pin(operand) for operand in operands])
    return pl.pallas_call(
        write_kernel,
        out_shape=outs,
        in_specs=[vmem, vmem],
        out_specs=(hbm, hbm),
        scratch_shapes=[dma((levels,)), dma],
        compiler_params=pltpu.CompilerParams(vmem_limit_bytes=8 << 20),
        name="write",
    )(solved, grad)


def solution(mesh):
    faces, tiles = mesh.shape["face"], mesh.shape["tile"]
    both = ("face", "tile")
    placed = (P(None, None, both, None),) + (P(None, both, None),) * 5 + (P(), P()) + (
        P(both, None, None), P(both, None), P(both))
    return jax.shard_map(
        functools.partial(per_device, faces, tiles),
        mesh=mesh,
        in_specs=placed,
        out_specs=(P(None, None, both, None), P(both, None, None)),
        check_vma=False,
    )
```

```python
import functools

import jax
import jax.numpy as jnp
from jax import lax
from jax.experimental import pallas as pl
from jax.experimental.pallas import tpu as pltpu
from jax.sharding import PartitionSpec as P

NI = 8
LANES = 128
SUB = 8
MESH = pl.DeviceIdType.MESH
F32 = jnp.float32
BF16 = jnp.bfloat16


def pieces(value, number):
    parts = []
    for _ in range(number):
        part = value.astype(BF16)
        parts.append(part)
        value = value - part.astype(F32)
    return parts


def column(c):
    return slice(c * LANES, (c + 1) * LANES)


def step_kernel(faces, tiles, ext_hbm, rot_hbm, sens_hbm, west_hbm, east_hbm, south_hbm, north_hbm,
                rate_hbm, regrid_hbm, owner_hbm, slot_hbm, solved, grad_ref,
                sens_v, west_v, east_v, south_v, north_v, rate_v, regrid_v, inverse_v, carry_v, upper_v,
                east_edge, west_edge, from_west, from_east, edge_rates, edge, flat, own_terms, their_terms, own_ids, their_ids,
                sums, in_b, sum_c, in_c,
                ext_ref, rot_ref, owner_ref, slot_ref, small_sem, level_sem, rate_sem, regrid_sem,
                east_send, east_recv, west_send, west_recv, ids_sem, send_a, recv_a, send_b, recv_b, send_c, recv_c):
    levels, species, rows, width = sens_v.shape
    chunks = width // LANES
    _, per_row, cells, inv_cells = regrid_v.shape
    blocks = rows * per_row
    lane_parts = cells // LANES
    group = SUB // species
    groups = levels // group
    face, tile = lax.axis_index("face"), lax.axis_index("tile")
    count, chips = faces * tiles, tiles // 2
    position = face * tiles + tile
    after, before = lax.rem(position + 1, count), lax.rem(position + count - 1, count)
    after = (after // tiles, lax.rem(after, tiles))
    before = (before // tiles, lax.rem(before, tiles))
    chip, core = tile // 2, lax.rem(tile, 2)
    partner = (face, tile + 1 - 2 * core)
    chip_of = [lax.rem(chip + step, chips) for step in range(chips)]
    face_of = [face]
    for step in range(1, faces):
        down, up = faces - step, step - 1
        down = down - (down <= face).astype(jnp.int32)
        up = up + (up >= face).astype(jnp.int32)
        face_of.append(jnp.where(face < faces // 2, down, up))
    others = [after, before, partner]
    others += [(face, 2 * chip_of[step] + core) for step in range(1, chips)]
    others += [(face_of[step], tile) for step in range(1, faces)]
    barrier = pltpu.get_barrier_semaphore()
    for other in others:
        pl.semaphore_signal(barrier, inc=1, device_id=other, device_id_type=MESH)

    def level_copies(level, pairs, base):
        return [
            pltpu.make_async_copy(source.at[level], sink.at[level], level_sem.at[base + number, level])
            for number, (source, sink) in enumerate(pairs)
        ]

    x_pairs = ((sens_hbm, sens_v), (west_hbm, west_v), (east_hbm, east_v))
    y_pairs = ((south_hbm, south_v), (north_hbm, north_v))
    rates = pltpu.make_async_copy(rate_hbm, rate_v.at[pl.ds(1, levels - 1)], rate_sem)

    def regrid_copy(part):
        return pltpu.make_async_copy(regrid_hbm.at[:, part], regrid_v.at[:, part], regrid_sem.at[part])

    small = [
        pltpu.make_async_copy(source, sink, small_sem.at[number])
        for number, (source, sink) in enumerate(
            ((ext_hbm, ext_ref), (rot_hbm, rot_ref), (owner_hbm, owner_ref), (slot_hbm, slot_ref)))
    ]
    for copy in small:
        copy.start()

    def start_group(part, pairs, base):
        for j in range(group):
            for copy in level_copies(part * group + j, pairs, base):
                copy.start()

    for part in range(groups):
        start_group(part, x_pairs, 0)

    for copy in small[:2]:
        copy.wait()
    rates.start()
    for part in range(groups):
        start_group(part, y_pairs, 3)
    extent = ext_ref[face, tile]
    row_ids = lax.broadcasted_iota(jnp.int32, (rows, LANES), 0)
    lane_ids = lax.broadcasted_iota(jnp.int32, (rows, LANES), 1)
    live = row_ids < extent
    first, last = row_ids == 0, row_ids == extent - 1
    west_live = jnp.logical_and(live, row_ids > 0)
    east_live = row_ids < extent - 1
    lane_first, lane_last = lane_ids == 0, lane_ids == LANES - 1
    zero = jnp.zeros((rows, LANES), F32)
    zero_field = jnp.zeros((rows, width), F32)
    rate_v[0] = zero_field
    rate_v[levels] = zero_field
    upper_v[0] = zero_field

    after_rotation = rot_ref[after[0], after[1]]
    my_rotation = rot_ref[face, tile]
    back = (lax.broadcasted_iota(jnp.int32, (LANES, LANES), 0)
            + lax.broadcasted_iota(jnp.int32, (LANES, LANES), 1) == LANES - 1)
    back = back.astype(F32).astype(BF16)
    edge_ids = lax.broadcasted_iota(jnp.int32, (SUB, LANES), 0)

    final_row = jnp.maximum(extent - 1, 0)
    final_rows = jnp.full((SUB, LANES), final_row, jnp.int32)
    final_low = final_rows < SUB
    to_row = [lax.rem(number + rows - final_row, SUB) for number in range(SUB)]

    def final_half(field):
        return jnp.where(final_low, field[:SUB], field[SUB:])

    def edge_copies(part):
        return (
            pltpu.make_async_remote_copy(
                src_ref=east_edge.at[part], dst_ref=from_west.at[part],
                send_sem=east_send.at[part], recv_sem=east_recv.at[part],
                device_id=after, device_id_type=MESH),
            pltpu.make_async_remote_copy(
                src_ref=west_edge.at[part], dst_ref=from_east.at[part],
                send_sem=west_send.at[part], recv_sem=west_recv.at[part],
                device_id=before, device_id_type=MESH),
        )

    def turn(values, rotation):
        straight = jnp.concatenate(values, axis=0)
        turned = sum(jnp.dot(piece, back, preferred_element_type=F32) for piece in pieces(straight, 3))
        reverse = jnp.full((SUB, LANES), rotation, jnp.int32) == 1
        return [
            jnp.where(reverse, turned[(chunks - 1 - c) * SUB:(chunks - c) * SUB], values[c])
            for c in range(chunks)
        ]

    hold = groups // 2

    def edges(part, carry):
        east_values, west_values = [None] * chunks, [None] * chunks
        for j in range(group):
            level = part * group + j
            for copy in level_copies(level, x_pairs, 0):
                copy.wait()


        @pl.when(part == 1)
        def _():
            for block in range(per_row):
                regrid_copy(block).start()

        for j in range(group):
            level = part * group + j
            for c in range(chunks):
                cols = column(c)
                east_half = final_half(east_v[level, :, cols])
                west_half = west_v[level, 0:SUB, cols]
                for kind in range(species):
                    value = sens_v[level, kind, :, cols]
                    east = east_half * final_half(value)
                    west = west_half * value[:SUB]
                    number = j * species + kind
                    east = pltpu.roll(east, to_row[number], 0)
                    if number == 0:
                        east_values[c], west_values[c] = east, west
                    else:
                        here = edge_ids == number
                        east_values[c] = jnp.where(here, east, east_values[c])
                        west_values[c] = jnp.where(here, pltpu.roll(west, number, 0), west_values[c])
        east_values = turn(east_values, after_rotation)
        west_values = turn(west_values, my_rotation)
        for c in range(chunks):
            east_edge[part, :, column(c)] = east_values[c]
            west_edge[part, :, column(c)] = west_values[c]

        @pl.when(part == hold)
        def _():
            pl.semaphore_wait(barrier, len(others))
            for sooner in range(hold):
                for copy in edge_copies(sooner):
                    copy.start()

        @pl.when(part >= hold)
        def _():
            for copy in edge_copies(part):
                copy.start()

        return carry

    lax.fori_loop(0, groups, edges, 0)
    for copy in small[2:]:
        copy.wait()
    half_k = own_ids.shape[1]
    block_of = lax.broadcasted_iota(jnp.int32, (blocks, half_k), 1)
    spare = block_of - blocks
    edge_row = jnp.where(lax.rem(spare, 2) == 0, 0, extent - 1)
    block_of = jnp.where(block_of < blocks, lax.rem(block_of, rows) * per_row + block_of // rows,
                         edge_row * per_row + spare // 2)
    permute = lax.broadcasted_iota(jnp.int32, (blocks, half_k), 0) == block_of
    permute = permute.astype(F32).astype(BF16)

    def permuted(ref):
        value = jnp.broadcast_to(ref[...].astype(F32), (SUB, blocks)).astype(BF16)
        return jnp.dot(value, permute, preferred_element_type=F32)

    ids = permuted(owner_ref) * float(NI) + permuted(slot_ref)
    spot_ids = lax.broadcasted_iota(jnp.int32, (SUB, half_k), 1)
    row_of, side_of = lax.rem(spot_ids, rows), lax.rem(spot_ids, 2)
    inner = jnp.logical_and(spot_ids < blocks, jnp.logical_and(row_of > 0, row_of != extent - 1))
    outer = jnp.logical_and(jnp.logical_and(spot_ids >= blocks, spot_ids < blocks + 2 * per_row),
                            jnp.logical_or(side_of == 0, extent > 1))
    own_ids[...] = jnp.where(jnp.logical_or(inner, outer), ids, -1.0)

    send_ids = pltpu.make_async_remote_copy(
        src_ref=own_ids, dst_ref=their_ids, send_sem=ids_sem.at[0], recv_sem=ids_sem.at[1],
        device_id=partner, device_id_type=MESH)
    send_ids.start()
    rates.wait()

    upper_half = edge_ids < species

    def edge_rows(field):
        tail = pltpu.roll(final_half(field), to_row[0], 0)
        return jnp.where(upper_half, jnp.broadcast_to(field[0:1], (SUB, LANES)),
                         jnp.broadcast_to(tail[0:1], (SUB, LANES)))

    def stencils(level, carry):
        for copy in level_copies(level, y_pairs, 3):
            copy.wait()

        held, behind = None, [zero] * species
        for c in range(chunks + 1):
            fresh = [(None, zero, zero)] * species
            if c < chunks:
                cols = column(c)
                west, east = west_v[level, :, cols], east_v[level, :, cols]
                south, north = south_v[level, :, cols], north_v[level, :, cols]
                keep_x = jnp.where(live, 1.0 - west - east, 0.0)
                west = jnp.where(west_live, west, 0.0)
                east = jnp.where(east_live, east, 0.0)
                keep_y = 1.0 - south - north
                fresh = []
                for kind in range(species):
                    value = sens_v[level, kind, :, cols]
                    moved = (keep_x * value + pltpu.roll(west * value, rows - 1, 0)
                             + pltpu.roll(east * value, 1, 0))
                    fresh.append((
                        keep_y * moved,
                        pltpu.roll(south * moved, LANES - 1, 1),
                        pltpu.roll(north * moved, 1, 1),
                    ))
                low, high = rate_v[level, :, cols], rate_v[level + 1, :, cols]
                inverse = 1.0 / ((1.0 + low + high) + low * upper_v[level, :, cols])
                upper = -high * inverse
                upper_v[level + 1, :, cols] = upper
                inverse_v[level, :, cols] = inverse
                carry_v[level, :, cols] = low * inverse
                for number, field in enumerate((south, north, inverse, low * inverse, upper)):
                    edge_rates[number, level, :, cols] = edge_rows(field)
            if c > 0:
                cols = column(c - 1)
                for kind in range(species):
                    centre, left, right = held[kind]
                    solved[level, kind, :, cols] = (
                        centre + jnp.where(lane_last, fresh[kind][1], left)
                        + jnp.where(lane_first, behind[kind], right))
                behind = [held[kind][2] for kind in range(species)]
            held = fresh
        return carry

    lax.fori_loop(0, levels, stencils, 0)

    used = (blocks + 2 * per_row) * species
    spare = jnp.zeros((own_terms.shape[0] - used, inv_cells), F32)
    own_terms[used:, :] = spare
    their_terms[used:, :] = spare

    def term_copy(part):
        if part < per_row:
            span = pl.ds(part * rows * species, rows * species)
        else:
            span = pl.ds(blocks * species, per_row * SUB)
        return pltpu.make_async_remote_copy(
            src_ref=own_terms.at[span], dst_ref=their_terms.at[span],
            send_sem=send_a.at[part], recv_sem=recv_a.at[part],
            device_id=partner, device_id_type=MESH)

    def solve(c, kind):
        cols = column(c)
        below, held = None, []
        for level in range(levels):
            value = solved[level, kind, :, cols] * inverse_v[level, :, cols]
            if level > 0:
                value = value + carry_v[level, :, cols] * below
            below = value
            held.append(value)
        for level in range(levels - 1, -1, -1):
            value = held[level]
            if level < levels - 1:
                value = value - upper_v[level + 1, :, cols] * below
            solved[level, kind, :, cols] = value
            below = value
        flat[c, pl.ds(kind, rows, stride=species), :] = below

    def units(part):
        spans = range(part * lane_parts, (part + 1) * lane_parts)
        return [(c, kind) for c in spans for kind in range(species)] if part < per_row else []

    def regridded(surface, weights):
        product = jnp.dot(surface.astype(BF16), jnp.concatenate(weights, axis=1), preferred_element_type=F32)
        value = product[:, :inv_cells]
        for j in range(1, len(weights)):
            value = jnp.where(edge_ids >= j * species, product[:, j * inv_cells:(j + 1) * inv_cells], value)
        return value

    for unit in units(0):
        solve(*unit)
    for part in range(per_row):
        regrid_copy(part).wait()
        ahead_units, pairs = units(part + 1), rows // group
        for pair in range(pairs):
            for unit in ahead_units[pair::pairs]:
                solve(*unit)
            lines = slice(pair * SUB, (pair + 1) * SUB)
            surface = jnp.concatenate(
                [flat[part * lane_parts + p, lines, :] for p in range(lane_parts)], axis=1)
            weights = [regrid_v[pair * group + j, part] for j in range(group)]
            start = part * rows * species + pair * SUB
            own_terms[start:start + SUB, :] = regridded(surface, weights)
        term_copy(part).start()

    small_first, small_last = lane_first[:SUB], lane_last[:SUB]
    nothing = jnp.zeros((SUB, LANES), F32)

    def edge_forward(part, carry):
        for copy in edge_copies(part):
            copy.wait_recv()
        for j in range(group):
            level = part * group + j
            previous = jnp.maximum(level - 1, 0)
            held, behind = None, nothing
            for c in range(chunks + 1):
                fresh = (None, nothing, nothing)
                if c < chunks:
                    cols = column(c)
                    south, north = edge_rates[0, level, :, cols], edge_rates[1, level, :, cols]
                    west, east = from_west[part, :, cols], from_east[part, :, cols]
                    if j > 0:
                        west = pltpu.roll(west, SUB - j * species, 0)
                    if j < group - 1:
                        east = pltpu.roll(east, SUB - (j + 1) * species, 0)
                    moved = jnp.where(upper_half, west, east)
                    fresh = ((1.0 - south - north) * moved,
                             pltpu.roll(south * moved, LANES - 1, 1), pltpu.roll(north * moved, 1, 1))
                if c > 0:
                    cols = column(c - 1)
                    centre, left, right = held
                    value = centre + jnp.where(small_last, fresh[1], left) + jnp.where(small_first, behind, right)
                    edge[level, :, cols] = (value * edge_rates[2, level, :, cols]
                                            + edge_rates[3, level, :, cols] * edge[previous, :, cols])
                    behind = right
                held = fresh
        return carry

    edge[0] = jnp.zeros((SUB, width), F32)
    lax.fori_loop(0, groups, edge_forward, 0)
    odd = lax.rem(final_rows, group) == 1
    lone = jnp.logical_and(upper_half, final_rows == 0)
    surfaces = []
    for c in range(chunks):
        cols = column(c)
        below = edge[levels - 1, :, cols]
        for level in range(levels - 2, -1, -1):
            below = edge[level, :, cols] - edge_rates[4, level, :, cols] * below
            edge[level, :, cols] = below
        slab = flat[c, 0:SUB, :]
        for pair in range(1, rows // group):
            slab = jnp.where(final_rows >= pair * group, flat[c, pair * SUB:(pair + 1) * SUB, :], slab)
        slab = jnp.where(odd, slab, pltpu.roll(slab, species, 0))
        below = below + jnp.where(lone, pltpu.roll(below, species, 0), 0.0)
        surfaces.append(below + jnp.where(upper_half, flat[c, 0:SUB, :], slab))
    for part in range(per_row):
        surface = jnp.concatenate(surfaces[part * lane_parts:(part + 1) * lane_parts], axis=1)
        start = blocks * species + part * SUB
        own_terms[start:start + SUB, :] = regridded(surface, [regrid_v[0, part], regrid_v[final_row, part]])
    term_copy(per_row).start()

    send_ids.wait_recv()
    unit = faces * NI
    height = chips * unit
    place = lax.broadcasted_iota(jnp.int32, (height, half_k), 0)
    to_chip = chip + place // unit
    to_chip = jnp.where(to_chip >= chips, to_chip - chips, to_chip)
    spot_of = lax.rem(place, unit) // NI
    to_face = jnp.full((height, half_k), face, jnp.int32)
    for spot in range(1, faces):
        to_face = jnp.where(spot_of == spot, face_of[spot], to_face)
    target = ((to_face * tiles + 2 * to_chip + core) * NI + lax.rem(place, NI)).astype(F32)
    select = jnp.concatenate(
        [(jnp.broadcast_to(ref[0:1, :], (height, half_k)) == target).astype(F32) for ref in (own_ids, their_ids)],
        axis=1).astype(BF16)
    for part in range(per_row + 1):
        term_copy(part).wait_recv()
    values = jnp.concatenate(
        [jnp.concatenate([ref[pl.ds(kind, half_k, stride=species), :] for kind in range(species)], axis=1)
         for ref in (own_terms, their_terms)], axis=0)
    total = sum(jnp.dot(select, piece, preferred_element_type=F32) for piece in pieces(values, 2))
    for step in range(chips):
        for spot in range(faces):
            start = step * unit + spot * NI
            sums[step, spot] = total[start:start + NI]

    spots = list(range(1, faces)) + [0]
    second, third = {}, {}
    for spot in spots:
        for step in range(1, chips):
            second[step, spot] = pltpu.make_async_remote_copy(
                src_ref=sums.at[step, spot], dst_ref=in_b.at[step - 1, spot],
                send_sem=send_b.at[step - 1, spot], recv_sem=recv_b.at[step - 1, spot],
                device_id=(face, 2 * chip_of[step] + core), device_id_type=MESH)
            second[step, spot].start()

    def add_edges(level, carry):
        for c in range(chunks):
            cols = column(c)
            for kind in range(species):
                solved[level, kind, :, cols] = (
                    solved[level, kind, :, cols] + jnp.where(first, edge[level, kind:kind + 1, cols], 0.0)
                    + jnp.where(last, edge[level, species + kind:species + kind + 1, cols], 0.0))
        return carry

    lax.fori_loop(0, levels, add_edges, 0)
    result = None
    for spot in spots:
        result = sums[0, spot]
        for step in range(1, chips):
            second[step, spot].wait_recv()
            result = result + in_b[step - 1, spot]
        if spot > 0:
            sum_c[spot - 1] = result
            third[spot] = pltpu.make_async_remote_copy(
                src_ref=sum_c.at[spot - 1], dst_ref=in_c.at[face],
                send_sem=send_c.at[spot - 1], recv_sem=recv_c.at[face],
                device_id=(face_of[spot], tile), device_id_type=MESH)
            third[spot].start()
    send_ids.wait_send()
    for part in range(groups):
        for copy in edge_copies(part):
            copy.wait_send()
    for part in range(per_row + 1):
        term_copy(part).wait_send()
    for copy in second.values():
        copy.wait_send()
    for spot in range(1, faces):
        pltpu.make_async_remote_copy(
            src_ref=sum_c.at[spot - 1], dst_ref=in_c.at[face_of[spot]],
            send_sem=send_c.at[spot - 1], recv_sem=recv_c.at[face_of[spot]],
            device_id=(face_of[spot], tile), device_id_type=MESH).wait_recv()
        result = result + in_c[face_of[spot]]
    for kind in range(species):
        grad_ref[:, kind, :] = result[:, kind * inv_cells:(kind + 1) * inv_cells]
    for copy in third.values():
        copy.wait_send()


def write_kernel(solved, grad, solved_out, grad_out, level_sem, grad_sem):
    copies = [pltpu.make_async_copy(grad, grad_out, grad_sem)]
    copies += [
        pltpu.make_async_copy(solved.at[level], solved_out.at[level], level_sem.at[level])
        for level in range(solved.shape[0])
    ]
    for copy in copies:
        copy.start()
    for copy in copies:
        copy.wait()


def per_device(faces, tiles, sensitivity, west_weight, east_weight, south_weight, north_weight,
               mixing_rate, extents, rotation, regrid_weight, owner, inv_slot):
    levels, species, rows, width = sensitivity.shape
    blocks, cells, inv_cells = regrid_weight.shape
    chips = tiles // 2
    hbm = pl.BlockSpec(memory_space=pltpu.HBM)
    vmem = pl.BlockSpec(memory_space=pltpu.VMEM)
    dma = pltpu.SemaphoreType.DMA
    groups = levels * species // SUB
    per_row = width // cells
    half_k = -(-(blocks + 2 * per_row) // LANES) * LANES
    field, line = (levels, rows, width), (groups, SUB, width)
    more = (levels + 1, rows, width)
    scratch = [pltpu.VMEM(shape, F32) for shape in [sensitivity.shape] + [field] * 4 + [more]]
    regrid_weight = regrid_weight.reshape(rows, per_row, cells, inv_cells)
    scratch += [pltpu.VMEM(regrid_weight.shape, regrid_weight.dtype)]
    shapes = [field, field, more] + [line] * 4 + [(5, levels, SUB, width), (levels, SUB, width)]
    shapes += [(width // LANES, rows * species, LANES)] + [(half_k * species, inv_cells)] * 2
    shapes += [(SUB, half_k)] * 2
    unit = (NI, species * inv_cells)
    shapes += [(chips, faces) + unit, (chips - 1, faces) + unit, (faces - 1,) + unit, (faces,) + unit]
    scratch += [pltpu.VMEM(shape, F32) for shape in shapes]
    scratch += [pltpu.SMEM(extents.shape, jnp.int32)] * 2 + [pltpu.VMEM((1, blocks), jnp.int32)] * 2
    scratch += [dma((4,)), dma((5, levels)), dma, dma((per_row,))]
    scratch += [dma((groups,))] * 4 + [dma((2,))] + [dma((per_row + 1,))] * 2
    scratch += [dma((chips - 1, faces))] * 2 + [dma((faces - 1,)), dma((faces,))]
    pin = functools.partial(pltpu.with_memory_space_constraint, memory_space=pltpu.HBM)
    operands = (extents, rotation, sensitivity, west_weight, east_weight, south_weight, north_weight,
                mixing_rate, regrid_weight, owner.reshape(1, blocks), inv_slot.reshape(1, blocks))
    outs = (
        jax.ShapeDtypeStruct(sensitivity.shape, F32),
        jax.ShapeDtypeStruct((NI, species, inv_cells), F32),
    )
    solved, grad = pl.pallas_call(
        functools.partial(step_kernel, faces, tiles),
        out_shape=outs,
        in_specs=[hbm] * 11,
        out_specs=(vmem, vmem),
        scratch_shapes=scratch,
        compiler_params=pltpu.CompilerParams(
            collective_id=0, has_side_effects=True, vmem_limit_bytes=44 << 20),
        name="step",
    )(*[pin(operand) for operand in operands])
    return pl.pallas_call(
        write_kernel,
        out_shape=outs,
        in_specs=[vmem, vmem],
        out_specs=(hbm, hbm),
        scratch_shapes=[dma((levels,)), dma],
        compiler_params=pltpu.CompilerParams(vmem_limit_bytes=8 << 20),
        name="write",
    )(solved, grad)


def solution(mesh):
    faces, tiles = mesh.shape["face"], mesh.shape["tile"]
    both = ("face", "tile")
    placed = (P(None, None, both, None),) + (P(None, both, None),) * 5 + (P(), P()) + (
        P(both, None, None), P(both, None), P(both))
    return jax.shard_map(
        functools.partial(per_device, faces, tiles),
        mesh=mesh,
        in_specs=placed,
        out_specs=(P(None, None, both, None), P(both, None, None)),
        check_vma=False,
    )
```

```python
import functools

import jax
import jax.numpy as jnp
from jax import lax
from jax.experimental import pallas as pl
from jax.experimental.pallas import tpu as pltpu
from jax.sharding import PartitionSpec as P

NI = 8
LANES = 128
SUB = 8
MESH = pl.DeviceIdType.MESH
F32 = jnp.float32
BF16 = jnp.bfloat16


def pieces(value, number):
    parts = []
    for _ in range(number):
        part = value.astype(BF16)
        parts.append(part)
        value = value - part.astype(F32)
    return parts


def column(c):
    return slice(c * LANES, (c + 1) * LANES)


def step_kernel(faces, tiles, ext_hbm, rot_hbm, sens_hbm, west_hbm, east_hbm, south_hbm, north_hbm,
                rate_hbm, regrid_hbm, owner_hbm, slot_hbm, solved, grad_ref,
                sens_v, west_v, east_v, south_v, north_v, rate_v, regrid_v, inverse_v, carry_v, upper_v,
                east_edge, west_edge, from_west, from_east, edge_rates, edge, flat, own_terms, their_terms, own_ids, their_ids,
                sums, in_b, sum_c, in_c,
                ext_ref, rot_ref, owner_ref, slot_ref, small_sem, level_sem, rate_sem, regrid_sem,
                east_send, east_recv, west_send, west_recv, ids_sem, send_a, recv_a, send_b, recv_b, send_c, recv_c):
    levels, species, rows, width = sens_v.shape
    chunks = width // LANES
    _, per_row, cells, inv_cells = regrid_v.shape
    blocks = rows * per_row
    lane_parts = cells // LANES
    group = SUB // species
    groups = levels // group
    face, tile = lax.axis_index("face"), lax.axis_index("tile")
    count, chips = faces * tiles, tiles // 2
    position = face * tiles + tile
    after, before = lax.rem(position + 1, count), lax.rem(position + count - 1, count)
    after = (after // tiles, lax.rem(after, tiles))
    before = (before // tiles, lax.rem(before, tiles))
    chip, core = tile // 2, lax.rem(tile, 2)
    partner = (face, tile + 1 - 2 * core)
    chip_of = [lax.rem(chip + step, chips) for step in range(chips)]
    face_of = [face]
    for step in range(1, faces):
        down, up = faces - step, step - 1
        down = down - (down <= face).astype(jnp.int32)
        up = up + (up >= face).astype(jnp.int32)
        face_of.append(jnp.where(face < faces // 2, down, up))
    others = [after, before, partner]
    others += [(face, 2 * chip_of[step] + core) for step in range(1, chips)]
    others += [(face_of[step], tile) for step in range(1, faces)]
    barrier = pltpu.get_barrier_semaphore()
    for other in others:
        pl.semaphore_signal(barrier, inc=1, device_id=other, device_id_type=MESH)

    def level_copies(level, pairs, base):
        return [
            pltpu.make_async_copy(source.at[level], sink.at[level], level_sem.at[base + number, level])
            for number, (source, sink) in enumerate(pairs)
        ]

    x_pairs = ((sens_hbm, sens_v), (west_hbm, west_v), (east_hbm, east_v))
    y_pairs = ((south_hbm, south_v), (north_hbm, north_v))
    rates = pltpu.make_async_copy(rate_hbm, rate_v.at[pl.ds(1, levels - 1)], rate_sem)

    def regrid_copy(part):
        return pltpu.make_async_copy(regrid_hbm.at[:, part], regrid_v.at[:, part], regrid_sem.at[part])

    small = [
        pltpu.make_async_copy(source, sink, small_sem.at[number])
        for number, (source, sink) in enumerate(
            ((ext_hbm, ext_ref), (rot_hbm, rot_ref), (owner_hbm, owner_ref), (slot_hbm, slot_ref)))
    ]
    for copy in small:
        copy.start()

    def start_group(part, pairs, base):
        for j in range(group):
            for copy in level_copies(part * group + j, pairs, base):
                copy.start()

    for part in range(groups):
        start_group(part, x_pairs, 0)

    for copy in small[:2]:
        copy.wait()
    rates.start()
    for part in range(groups):
        start_group(part, y_pairs, 3)
    extent = ext_ref[face, tile]
    row_ids = lax.broadcasted_iota(jnp.int32, (rows, LANES), 0)
    lane_ids = lax.broadcasted_iota(jnp.int32, (rows, LANES), 1)
    live = row_ids < extent
    first, last = row_ids == 0, row_ids == extent - 1
    west_live = jnp.logical_and(live, row_ids > 0)
    east_live = row_ids < extent - 1
    lane_first, lane_last = lane_ids == 0, lane_ids == LANES - 1
    zero = jnp.zeros((rows, LANES), F32)
    zero_field = jnp.zeros((rows, width), F32)
    rate_v[0] = zero_field
    rate_v[levels] = zero_field
    upper_v[0] = zero_field

    after_rotation = rot_ref[after[0], after[1]]
    my_rotation = rot_ref[face, tile]
    back = (lax.broadcasted_iota(jnp.int32, (LANES, LANES), 0)
            + lax.broadcasted_iota(jnp.int32, (LANES, LANES), 1) == LANES - 1)
    back = back.astype(F32).astype(BF16)
    edge_ids = lax.broadcasted_iota(jnp.int32, (SUB, LANES), 0)

    final_row = jnp.maximum(extent - 1, 0)
    final_rows = jnp.full((SUB, LANES), final_row, jnp.int32)
    final_low = final_rows < SUB
    to_row = [lax.rem(number + rows - final_row, SUB) for number in range(SUB)]

    def final_half(field):
        return jnp.where(final_low, field[:SUB], field[SUB:])

    def edge_copies(part):
        return (
            pltpu.make_async_remote_copy(
                src_ref=east_edge.at[part], dst_ref=from_west.at[part],
                send_sem=east_send.at[part], recv_sem=east_recv.at[part],
                device_id=after, device_id_type=MESH),
            pltpu.make_async_remote_copy(
                src_ref=west_edge.at[part], dst_ref=from_east.at[part],
                send_sem=west_send.at[part], recv_sem=west_recv.at[part],
                device_id=before, device_id_type=MESH),
        )

    def turn(values, rotation):
        straight = jnp.concatenate(values, axis=0)
        turned = sum(jnp.dot(piece, back, preferred_element_type=F32) for piece in pieces(straight, 3))
        reverse = jnp.full((SUB, LANES), rotation, jnp.int32) == 1
        return [
            jnp.where(reverse, turned[(chunks - 1 - c) * SUB:(chunks - c) * SUB], values[c])
            for c in range(chunks)
        ]

    hold = groups // 2

    def edges(part, carry):
        east_values, west_values = [None] * chunks, [None] * chunks
        for j in range(group):
            level = part * group + j
            for copy in level_copies(level, x_pairs, 0):
                copy.wait()


        @pl.when(part == 1)
        def _():
            for block in range(per_row):
                regrid_copy(block).start()

        for j in range(group):
            level = part * group + j
            for c in range(chunks):
                cols = column(c)
                east_half = final_half(east_v[level, :, cols])
                west_half = west_v[level, 0:SUB, cols]
                for kind in range(species):
                    value = sens_v[level, kind, :, cols]
                    east = east_half * final_half(value)
                    west = west_half * value[:SUB]
                    number = j * species + kind
                    east = pltpu.roll(east, to_row[number], 0)
                    if number == 0:
                        east_values[c], west_values[c] = east, west
                    else:
                        here = edge_ids == number
                        east_values[c] = jnp.where(here, east, east_values[c])
                        west_values[c] = jnp.where(here, pltpu.roll(west, number, 0), west_values[c])
        east_values = turn(east_values, after_rotation)
        west_values = turn(west_values, my_rotation)
        for c in range(chunks):
            east_edge[part, :, column(c)] = east_values[c]
            west_edge[part, :, column(c)] = west_values[c]

        @pl.when(part == hold)
        def _():
            pl.semaphore_wait(barrier, len(others))
            for sooner in range(hold):
                for copy in edge_copies(sooner):
                    copy.start()

        @pl.when(part >= hold)
        def _():
            for copy in edge_copies(part):
                copy.start()

        return carry

    lax.fori_loop(0, groups, edges, 0)
    for copy in small[2:]:
        copy.wait()
    half_k = own_ids.shape[1]
    block_of = lax.broadcasted_iota(jnp.int32, (blocks, half_k), 1)
    spare = block_of - blocks
    edge_row = jnp.where(lax.rem(spare, 2) == 0, 0, extent - 1)
    block_of = jnp.where(block_of < blocks, lax.rem(block_of, rows) * per_row + block_of // rows,
                         edge_row * per_row + spare // 2)
    permute = lax.broadcasted_iota(jnp.int32, (blocks, half_k), 0) == block_of
    permute = permute.astype(F32).astype(BF16)

    def permuted(ref):
        value = jnp.broadcast_to(ref[...].astype(F32), (SUB, blocks)).astype(BF16)
        return jnp.dot(value, permute, preferred_element_type=F32)

    ids = permuted(owner_ref) * float(NI) + permuted(slot_ref)
    spot_ids = lax.broadcasted_iota(jnp.int32, (SUB, half_k), 1)
    row_of, side_of = lax.rem(spot_ids, rows), lax.rem(spot_ids, 2)
    inner = jnp.logical_and(spot_ids < blocks, jnp.logical_and(row_of > 0, row_of != extent - 1))
    outer = jnp.logical_and(jnp.logical_and(spot_ids >= blocks, spot_ids < blocks + 2 * per_row),
                            jnp.logical_or(side_of == 0, extent > 1))
    own_ids[...] = jnp.where(jnp.logical_or(inner, outer), ids, -1.0)

    send_ids = pltpu.make_async_remote_copy(
        src_ref=own_ids, dst_ref=their_ids, send_sem=ids_sem.at[0], recv_sem=ids_sem.at[1],
        device_id=partner, device_id_type=MESH)
    send_ids.start()
    rates.wait()

    upper_half = edge_ids < species

    def edge_rows(field):
        tail = pltpu.roll(final_half(field), to_row[0], 0)
        return jnp.where(upper_half, jnp.broadcast_to(field[0:1], (SUB, LANES)),
                         jnp.broadcast_to(tail[0:1], (SUB, LANES)))

    def stencils(level, carry):
        for copy in level_copies(level, y_pairs, 3):
            copy.wait()

        held, behind = None, [zero] * species
        for c in range(chunks + 1):
            fresh = [(None, zero, zero)] * species
            if c < chunks:
                cols = column(c)
                west, east = west_v[level, :, cols], east_v[level, :, cols]
                south, north = south_v[level, :, cols], north_v[level, :, cols]
                keep_x = jnp.where(live, 1.0 - west - east, 0.0)
                west = jnp.where(west_live, west, 0.0)
                east = jnp.where(east_live, east, 0.0)
                keep_y = 1.0 - south - north
                fresh = []
                for kind in range(species):
                    value = sens_v[level, kind, :, cols]
                    moved = (keep_x * value + pltpu.roll(west * value, rows - 1, 0)
                             + pltpu.roll(east * value, 1, 0))
                    fresh.append((
                        keep_y * moved,
                        pltpu.roll(south * moved, LANES - 1, 1),
                        pltpu.roll(north * moved, 1, 1),
                    ))
                low, high = rate_v[level, :, cols], rate_v[level + 1, :, cols]
                inverse = 1.0 / ((1.0 + low + high) + low * upper_v[level, :, cols])
                upper = -high * inverse
                upper_v[level + 1, :, cols] = upper
                inverse_v[level, :, cols] = inverse
                carry_v[level, :, cols] = low * inverse
                for number, field in enumerate((south, north, inverse, low * inverse, upper)):
                    edge_rates[number, level, :, cols] = edge_rows(field)
            if c > 0:
                cols = column(c - 1)
                for kind in range(species):
                    centre, left, right = held[kind]
                    solved[level, kind, :, cols] = (
                        centre + jnp.where(lane_last, fresh[kind][1], left)
                        + jnp.where(lane_first, behind[kind], right))
                behind = [held[kind][2] for kind in range(species)]
            held = fresh
        return carry

    lax.fori_loop(0, levels, stencils, 0)

    used = (blocks + 2 * per_row) * species
    spare = jnp.zeros((own_terms.shape[0] - used, inv_cells), F32)
    own_terms[used:, :] = spare
    their_terms[used:, :] = spare

    def term_copy(part):
        if part < per_row:
            span = pl.ds(part * rows * species, rows * species)
        else:
            span = pl.ds(blocks * species, per_row * SUB)
        return pltpu.make_async_remote_copy(
            src_ref=own_terms.at[span], dst_ref=their_terms.at[span],
            send_sem=send_a.at[part], recv_sem=recv_a.at[part],
            device_id=partner, device_id_type=MESH)

    def solve(c, kind):
        cols = column(c)
        below, held = None, []
        for level in range(levels):
            value = solved[level, kind, :, cols] * inverse_v[level, :, cols]
            if level > 0:
                value = value + carry_v[level, :, cols] * below
            below = value
            held.append(value)
        for level in range(levels - 1, -1, -1):
            value = held[level]
            if level < levels - 1:
                value = value - upper_v[level + 1, :, cols] * below
            solved[level, kind, :, cols] = value
            below = value
        flat[c, pl.ds(kind, rows, stride=species), :] = below

    def units(part):
        spans = range(part * lane_parts, (part + 1) * lane_parts)
        return [(c, kind) for c in spans for kind in range(species)] if part < per_row else []

    def regridded(surface, weights):
        product = jnp.dot(surface.astype(BF16), jnp.concatenate(weights, axis=1), preferred_element_type=F32)
        value = product[:, :inv_cells]
        for j in range(1, len(weights)):
            value = jnp.where(edge_ids >= j * species, product[:, j * inv_cells:(j + 1) * inv_cells], value)
        return value

    for unit in units(0):
        solve(*unit)
    for part in range(per_row):
        regrid_copy(part).wait()
        ahead_units, pairs = units(part + 1), rows // group
        for pair in range(pairs):
            for unit in ahead_units[pair::pairs]:
                solve(*unit)
            lines = slice(pair * SUB, (pair + 1) * SUB)
            surface = jnp.concatenate(
                [flat[part * lane_parts + p, lines, :] for p in range(lane_parts)], axis=1)
            weights = [regrid_v[pair * group + j, part] for j in range(group)]
            start = part * rows * species + pair * SUB
            own_terms[start:start + SUB, :] = regridded(surface, weights)
        term_copy(part).start()

    small_first, small_last = lane_first[:SUB], lane_last[:SUB]
    nothing = jnp.zeros((SUB, LANES), F32)

    def edge_forward(part):
        for copy in edge_copies(part):
            copy.wait_recv()
        for j in range(group):
            level = part * group + j
            held, behind = None, nothing
            for c in range(chunks + 1):
                fresh = (None, nothing, nothing)
                if c < chunks:
                    cols = column(c)
                    south, north = edge_rates[0, level, :, cols], edge_rates[1, level, :, cols]
                    west, east = from_west[part, :, cols], from_east[part, :, cols]
                    if j > 0:
                        west = pltpu.roll(west, SUB - j * species, 0)
                    if j < group - 1:
                        east = pltpu.roll(east, SUB - (j + 1) * species, 0)
                    moved = jnp.where(upper_half, west, east)
                    fresh = ((1.0 - south - north) * moved,
                             pltpu.roll(south * moved, LANES - 1, 1), pltpu.roll(north * moved, 1, 1))
                if c > 0:
                    cols = column(c - 1)
                    centre, left, right = held
                    value = centre + jnp.where(small_last, fresh[1], left) + jnp.where(small_first, behind, right)
                    value = value * edge_rates[2, level, :, cols]
                    if level > 0:
                        value = value + edge_rates[3, level, :, cols] * edge[level - 1, :, cols]
                    edge[level, :, cols] = value
                    behind = right
                held = fresh

    for part in range(groups):
        edge_forward(part)
    odd = lax.rem(final_rows, group) == 1
    lone = jnp.logical_and(upper_half, final_rows == 0)
    surfaces = []
    for c in range(chunks):
        cols = column(c)
        below = edge[levels - 1, :, cols]
        for level in range(levels - 2, -1, -1):
            below = edge[level, :, cols] - edge_rates[4, level, :, cols] * below
            edge[level, :, cols] = below
        slab = flat[c, 0:SUB, :]
        for pair in range(1, rows // group):
            slab = jnp.where(final_rows >= pair * group, flat[c, pair * SUB:(pair + 1) * SUB, :], slab)
        slab = jnp.where(odd, slab, pltpu.roll(slab, species, 0))
        below = below + jnp.where(lone, pltpu.roll(below, species, 0), 0.0)
        surfaces.append(below + jnp.where(upper_half, flat[c, 0:SUB, :], slab))
    for part in range(per_row):
        surface = jnp.concatenate(surfaces[part * lane_parts:(part + 1) * lane_parts], axis=1)
        start = blocks * species + part * SUB
        own_terms[start:start + SUB, :] = regridded(surface, [regrid_v[0, part], regrid_v[final_row, part]])
    term_copy(per_row).start()

    send_ids.wait_recv()
    unit = faces * NI
    height = chips * unit
    place = lax.broadcasted_iota(jnp.int32, (height, half_k), 0)
    to_chip = chip + place // unit
    to_chip = jnp.where(to_chip >= chips, to_chip - chips, to_chip)
    spot_of = lax.rem(place, unit) // NI
    to_face = jnp.full((height, half_k), face, jnp.int32)
    for spot in range(1, faces):
        to_face = jnp.where(spot_of == spot, face_of[spot], to_face)
    target = ((to_face * tiles + 2 * to_chip + core) * NI + lax.rem(place, NI)).astype(F32)
    select = jnp.concatenate(
        [(jnp.broadcast_to(ref[0:1, :], (height, half_k)) == target).astype(F32) for ref in (own_ids, their_ids)],
        axis=1).astype(BF16)
    for part in range(per_row + 1):
        term_copy(part).wait_recv()
    values = jnp.concatenate(
        [jnp.concatenate([ref[pl.ds(kind, half_k, stride=species), :] for kind in range(species)], axis=1)
         for ref in (own_terms, their_terms)], axis=0)
    total = sum(jnp.dot(select, piece, preferred_element_type=F32) for piece in pieces(values, 2))
    for step in range(chips):
        for spot in range(faces):
            start = step * unit + spot * NI
            sums[step, spot] = total[start:start + NI]

    spots = list(range(1, faces)) + [0]
    second, third = {}, {}
    for spot in spots:
        for step in range(1, chips):
            second[step, spot] = pltpu.make_async_remote_copy(
                src_ref=sums.at[step, spot], dst_ref=in_b.at[step - 1, spot],
                send_sem=send_b.at[step - 1, spot], recv_sem=recv_b.at[step - 1, spot],
                device_id=(face, 2 * chip_of[step] + core), device_id_type=MESH)
            second[step, spot].start()

    def add_edges(level, carry):
        for c in range(chunks):
            cols = column(c)
            for kind in range(species):
                solved[level, kind, :, cols] = (
                    solved[level, kind, :, cols] + jnp.where(first, edge[level, kind:kind + 1, cols], 0.0)
                    + jnp.where(last, edge[level, species + kind:species + kind + 1, cols], 0.0))
        return carry

    lax.fori_loop(0, levels, add_edges, 0)
    result = None
    for spot in spots:
        result = sums[0, spot]
        for step in range(1, chips):
            second[step, spot].wait_recv()
            result = result + in_b[step - 1, spot]
        if spot > 0:
            sum_c[spot - 1] = result
            third[spot] = pltpu.make_async_remote_copy(
                src_ref=sum_c.at[spot - 1], dst_ref=in_c.at[face],
                send_sem=send_c.at[spot - 1], recv_sem=recv_c.at[face],
                device_id=(face_of[spot], tile), device_id_type=MESH)
            third[spot].start()
    send_ids.wait_send()
    for part in range(groups):
        for copy in edge_copies(part):
            copy.wait_send()
    for part in range(per_row + 1):
        term_copy(part).wait_send()
    for copy in second.values():
        copy.wait_send()
    for spot in range(1, faces):
        pltpu.make_async_remote_copy(
            src_ref=sum_c.at[spot - 1], dst_ref=in_c.at[face_of[spot]],
            send_sem=send_c.at[spot - 1], recv_sem=recv_c.at[face_of[spot]],
            device_id=(face_of[spot], tile), device_id_type=MESH).wait_recv()
        result = result + in_c[face_of[spot]]
    for kind in range(species):
        grad_ref[:, kind, :] = result[:, kind * inv_cells:(kind + 1) * inv_cells]
    for copy in third.values():
        copy.wait_send()


def write_kernel(solved, grad, solved_out, grad_out, level_sem, grad_sem):
    copies = [pltpu.make_async_copy(grad, grad_out, grad_sem)]
    copies += [
        pltpu.make_async_copy(solved.at[level], solved_out.at[level], level_sem.at[level])
        for level in range(solved.shape[0])
    ]
    for copy in copies:
        copy.start()
    for copy in copies:
        copy.wait()


def per_device(faces, tiles, sensitivity, west_weight, east_weight, south_weight, north_weight,
               mixing_rate, extents, rotation, regrid_weight, owner, inv_slot):
    levels, species, rows, width = sensitivity.shape
    blocks, cells, inv_cells = regrid_weight.shape
    chips = tiles // 2
    hbm = pl.BlockSpec(memory_space=pltpu.HBM)
    vmem = pl.BlockSpec(memory_space=pltpu.VMEM)
    dma = pltpu.SemaphoreType.DMA
    groups = levels * species // SUB
    per_row = width // cells
    half_k = -(-(blocks + 2 * per_row) // LANES) * LANES
    field, line = (levels, rows, width), (groups, SUB, width)
    more = (levels + 1, rows, width)
    scratch = [pltpu.VMEM(shape, F32) for shape in [sensitivity.shape] + [field] * 4 + [more]]
    regrid_weight = regrid_weight.reshape(rows, per_row, cells, inv_cells)
    scratch += [pltpu.VMEM(regrid_weight.shape, regrid_weight.dtype)]
    shapes = [field, field, more] + [line] * 4 + [(5, levels, SUB, width), (levels, SUB, width)]
    shapes += [(width // LANES, rows * species, LANES)] + [(half_k * species, inv_cells)] * 2
    shapes += [(SUB, half_k)] * 2
    unit = (NI, species * inv_cells)
    shapes += [(chips, faces) + unit, (chips - 1, faces) + unit, (faces - 1,) + unit, (faces,) + unit]
    scratch += [pltpu.VMEM(shape, F32) for shape in shapes]
    scratch += [pltpu.SMEM(extents.shape, jnp.int32)] * 2 + [pltpu.VMEM((1, blocks), jnp.int32)] * 2
    scratch += [dma((4,)), dma((5, levels)), dma, dma((per_row,))]
    scratch += [dma((groups,))] * 4 + [dma((2,))] + [dma((per_row + 1,))] * 2
    scratch += [dma((chips - 1, faces))] * 2 + [dma((faces - 1,)), dma((faces,))]
    pin = functools.partial(pltpu.with_memory_space_constraint, memory_space=pltpu.HBM)
    operands = (extents, rotation, sensitivity, west_weight, east_weight, south_weight, north_weight,
                mixing_rate, regrid_weight, owner.reshape(1, blocks), inv_slot.reshape(1, blocks))
    outs = (
        jax.ShapeDtypeStruct(sensitivity.shape, F32),
        jax.ShapeDtypeStruct((NI, species, inv_cells), F32),
    )
    solved, grad = pl.pallas_call(
        functools.partial(step_kernel, faces, tiles),
        out_shape=outs,
        in_specs=[hbm] * 11,
        out_specs=(vmem, vmem),
        scratch_shapes=scratch,
        compiler_params=pltpu.CompilerParams(
            collective_id=0, has_side_effects=True, vmem_limit_bytes=44 << 20),
        name="step",
    )(*[pin(operand) for operand in operands])
    return pl.pallas_call(
        write_kernel,
        out_shape=outs,
        in_specs=[vmem, vmem],
        out_specs=(hbm, hbm),
        scratch_shapes=[dma((levels,)), dma],
        compiler_params=pltpu.CompilerParams(vmem_limit_bytes=8 << 20),
        name="write",
    )(solved, grad)


def solution(mesh):
    faces, tiles = mesh.shape["face"], mesh.shape["tile"]
    both = ("face", "tile")
    placed = (P(None, None, both, None),) + (P(None, both, None),) * 5 + (P(), P()) + (
        P(both, None, None), P(both, None), P(both))
    return jax.shard_map(
        functools.partial(per_device, faces, tiles),
        mesh=mesh,
        in_specs=placed,
        out_specs=(P(None, None, both, None), P(both, None, None)),
        check_vma=False,
    )
```

```python
import functools

import jax
import jax.numpy as jnp
from jax import lax
from jax.experimental import pallas as pl
from jax.experimental.pallas import tpu as pltpu
from jax.sharding import PartitionSpec as P

NI = 8
LANES = 128
SUB = 8
MESH = pl.DeviceIdType.MESH
F32 = jnp.float32
BF16 = jnp.bfloat16


def pieces(value, number):
    parts = []
    for _ in range(number):
        part = value.astype(BF16)
        parts.append(part)
        value = value - part.astype(F32)
    return parts


def column(c):
    return slice(c * LANES, (c + 1) * LANES)


def step_kernel(faces, tiles, ext_hbm, rot_hbm, sens_hbm, west_hbm, east_hbm, south_hbm, north_hbm,
                rate_hbm, regrid_hbm, owner_hbm, slot_hbm, solved, grad_ref,
                sens_v, west_v, east_v, south_v, north_v, rate_v, regrid_v, inverse_v, carry_v, upper_v,
                east_edge, west_edge, from_west, from_east, edge_rates, edge, flat, own_terms, their_terms, own_ids, their_ids,
                sums, in_b, sum_c, in_c,
                ext_ref, rot_ref, owner_ref, slot_ref, small_sem, level_sem, rate_sem, regrid_sem,
                east_send, east_recv, west_send, west_recv, ids_sem, send_a, recv_a, send_b, recv_b, send_c, recv_c):
    levels, species, rows, width = sens_v.shape
    chunks = width // LANES
    _, per_row, cells, inv_cells = regrid_v.shape
    blocks = rows * per_row
    lane_parts = cells // LANES
    group = SUB // species
    groups = levels // group
    face, tile = lax.axis_index("face"), lax.axis_index("tile")
    count, chips = faces * tiles, tiles // 2
    position = face * tiles + tile
    after, before = lax.rem(position + 1, count), lax.rem(position + count - 1, count)
    after = (after // tiles, lax.rem(after, tiles))
    before = (before // tiles, lax.rem(before, tiles))
    chip, core = tile // 2, lax.rem(tile, 2)
    partner = (face, tile + 1 - 2 * core)
    chip_of = [lax.rem(chip + step, chips) for step in range(chips)]
    face_of = [face]
    for step in range(1, faces):
        down, up = faces - step, step - 1
        down = down - (down <= face).astype(jnp.int32)
        up = up + (up >= face).astype(jnp.int32)
        face_of.append(jnp.where(face < faces // 2, down, up))
    others = [after, before, partner]
    others += [(face, 2 * chip_of[step] + core) for step in range(1, chips)]
    others += [(face_of[step], tile) for step in range(1, faces)]
    barrier = pltpu.get_barrier_semaphore()
    for other in others:
        pl.semaphore_signal(barrier, inc=1, device_id=other, device_id_type=MESH)

    def level_copies(level, pairs, base):
        return [
            pltpu.make_async_copy(source.at[level], sink.at[level], level_sem.at[base + number, level])
            for number, (source, sink) in enumerate(pairs)
        ]

    x_pairs = ((sens_hbm, sens_v), (west_hbm, west_v), (east_hbm, east_v))
    y_pairs = ((south_hbm, south_v), (north_hbm, north_v))
    rates = pltpu.make_async_copy(rate_hbm, rate_v.at[pl.ds(1, levels - 1)], rate_sem)

    def regrid_copy(part):
        return pltpu.make_async_copy(regrid_hbm.at[:, part], regrid_v.at[:, part], regrid_sem.at[part])

    small = [
        pltpu.make_async_copy(source, sink, small_sem.at[number])
        for number, (source, sink) in enumerate(
            ((ext_hbm, ext_ref), (rot_hbm, rot_ref), (owner_hbm, owner_ref), (slot_hbm, slot_ref)))
    ]
    for copy in small:
        copy.start()

    def start_group(part, pairs, base):
        for j in range(group):
            for copy in level_copies(part * group + j, pairs, base):
                copy.start()

    for part in range(groups):
        start_group(part, x_pairs, 0)

    for copy in small[:2]:
        copy.wait()
    rates.start()
    for part in range(groups):
        start_group(part, y_pairs, 3)
    extent = ext_ref[face, tile]
    row_ids = lax.broadcasted_iota(jnp.int32, (rows, LANES), 0)
    lane_ids = lax.broadcasted_iota(jnp.int32, (rows, LANES), 1)
    live = row_ids < extent
    first, last = row_ids == 0, row_ids == extent - 1
    west_live = jnp.logical_and(live, row_ids > 0)
    east_live = row_ids < extent - 1
    lane_first, lane_last = lane_ids == 0, lane_ids == LANES - 1
    zero = jnp.zeros((rows, LANES), F32)
    zero_field = jnp.zeros((rows, width), F32)
    rate_v[0] = zero_field
    rate_v[levels] = zero_field
    upper_v[0] = zero_field

    after_rotation = rot_ref[after[0], after[1]]
    my_rotation = rot_ref[face, tile]
    back = (lax.broadcasted_iota(jnp.int32, (LANES, LANES), 0)
            + lax.broadcasted_iota(jnp.int32, (LANES, LANES), 1) == LANES - 1)
    back = back.astype(F32).astype(BF16)
    edge_ids = lax.broadcasted_iota(jnp.int32, (SUB, LANES), 0)

    final_row = jnp.maximum(extent - 1, 0)
    final_rows = jnp.full((SUB, LANES), final_row, jnp.int32)
    final_low = final_rows < SUB
    to_row = [lax.rem(number + rows - final_row, SUB) for number in range(SUB)]

    def final_half(field):
        return jnp.where(final_low, field[:SUB], field[SUB:])

    def edge_copies(part):
        return (
            pltpu.make_async_remote_copy(
                src_ref=east_edge.at[part], dst_ref=from_west.at[part],
                send_sem=east_send.at[part], recv_sem=east_recv.at[part],
                device_id=after, device_id_type=MESH),
            pltpu.make_async_remote_copy(
                src_ref=west_edge.at[part], dst_ref=from_east.at[part],
                send_sem=west_send.at[part], recv_sem=west_recv.at[part],
                device_id=before, device_id_type=MESH),
        )

    def turn(values, rotation):
        straight = jnp.concatenate(values, axis=0)
        turned = sum(jnp.dot(piece, back, preferred_element_type=F32) for piece in pieces(straight, 3))
        reverse = jnp.full((SUB, LANES), rotation, jnp.int32) == 1
        return [
            jnp.where(reverse, turned[(chunks - 1 - c) * SUB:(chunks - c) * SUB], values[c])
            for c in range(chunks)
        ]

    hold = groups // 2

    def edges(part, carry):
        east_values, west_values = [None] * chunks, [None] * chunks
        for j in range(group):
            level = part * group + j
            for copy in level_copies(level, x_pairs, 0):
                copy.wait()


        @pl.when(part == 1)
        def _():
            for block in range(per_row):
                regrid_copy(block).start()

        for j in range(group):
            level = part * group + j
            for c in range(chunks):
                cols = column(c)
                east_half = final_half(east_v[level, :, cols])
                west_half = west_v[level, 0:SUB, cols]
                for kind in range(species):
                    value = sens_v[level, kind, :, cols]
                    east = east_half * final_half(value)
                    west = west_half * value[:SUB]
                    number = j * species + kind
                    east = pltpu.roll(east, to_row[number], 0)
                    if number == 0:
                        east_values[c], west_values[c] = east, west
                    else:
                        here = edge_ids == number
                        east_values[c] = jnp.where(here, east, east_values[c])
                        west_values[c] = jnp.where(here, pltpu.roll(west, number, 0), west_values[c])
        east_values = turn(east_values, after_rotation)
        west_values = turn(west_values, my_rotation)
        for c in range(chunks):
            east_edge[part, :, column(c)] = east_values[c]
            west_edge[part, :, column(c)] = west_values[c]

        @pl.when(part == hold)
        def _():
            pl.semaphore_wait(barrier, len(others))
            for sooner in range(hold):
                for copy in edge_copies(sooner):
                    copy.start()

        @pl.when(part >= hold)
        def _():
            for copy in edge_copies(part):
                copy.start()

        return carry

    lax.fori_loop(0, groups, edges, 0)
    for copy in small[2:]:
        copy.wait()
    half_k = own_ids.shape[1]
    block_of = lax.broadcasted_iota(jnp.int32, (blocks, half_k), 1)
    spare = block_of - blocks
    edge_row = jnp.where(lax.rem(spare, 2) == 0, 0, extent - 1)
    block_of = jnp.where(block_of < blocks, lax.rem(block_of, rows) * per_row + block_of // rows,
                         edge_row * per_row + spare // 2)
    permute = lax.broadcasted_iota(jnp.int32, (blocks, half_k), 0) == block_of
    permute = permute.astype(F32).astype(BF16)

    def permuted(ref):
        value = jnp.broadcast_to(ref[...].astype(F32), (SUB, blocks)).astype(BF16)
        return jnp.dot(value, permute, preferred_element_type=F32)

    ids = permuted(owner_ref) * float(NI) + permuted(slot_ref)
    spot_ids = lax.broadcasted_iota(jnp.int32, (SUB, half_k), 1)
    row_of, side_of = lax.rem(spot_ids, rows), lax.rem(spot_ids, 2)
    inner = jnp.logical_and(spot_ids < blocks, jnp.logical_and(row_of > 0, row_of != extent - 1))
    outer = jnp.logical_and(jnp.logical_and(spot_ids >= blocks, spot_ids < blocks + 2 * per_row),
                            jnp.logical_or(side_of == 0, extent > 1))
    own_ids[...] = jnp.where(jnp.logical_or(inner, outer), ids, -1.0)

    send_ids = pltpu.make_async_remote_copy(
        src_ref=own_ids, dst_ref=their_ids, send_sem=ids_sem.at[0], recv_sem=ids_sem.at[1],
        device_id=partner, device_id_type=MESH)
    send_ids.start()
    rates.wait()

    upper_half = edge_ids < species

    def edge_rows(field):
        tail = pltpu.roll(final_half(field), to_row[0], 0)
        return jnp.where(upper_half, jnp.broadcast_to(field[0:1], (SUB, LANES)),
                         jnp.broadcast_to(tail[0:1], (SUB, LANES)))

    def stencils(level, carry):
        for copy in level_copies(level, y_pairs, 3):
            copy.wait()

        held, behind = None, [zero] * species
        for c in range(chunks + 1):
            fresh = [(None, zero, zero)] * species
            if c < chunks:
                cols = column(c)
                west, east = west_v[level, :, cols], east_v[level, :, cols]
                south, north = south_v[level, :, cols], north_v[level, :, cols]
                keep_x = jnp.where(live, 1.0 - west - east, 0.0)
                west = jnp.where(west_live, west, 0.0)
                east = jnp.where(east_live, east, 0.0)
                keep_y = 1.0 - south - north
                fresh = []
                for kind in range(species):
                    value = sens_v[level, kind, :, cols]
                    moved = (keep_x * value + pltpu.roll(west * value, rows - 1, 0)
                             + pltpu.roll(east * value, 1, 0))
                    fresh.append((
                        keep_y * moved,
                        pltpu.roll(south * moved, LANES - 1, 1),
                        pltpu.roll(north * moved, 1, 1),
                    ))
                low, high = rate_v[level, :, cols], rate_v[level + 1, :, cols]
                inverse = 1.0 / ((1.0 + low + high) + low * upper_v[level, :, cols])
                upper = -high * inverse
                upper_v[level + 1, :, cols] = upper
                inverse_v[level, :, cols] = inverse
                carry_v[level, :, cols] = low * inverse
                for number, field in enumerate((south, north, inverse, low * inverse, upper)):
                    edge_rates[number, level, :, cols] = edge_rows(field)
            if c > 0:
                cols = column(c - 1)
                for kind in range(species):
                    centre, left, right = held[kind]
                    solved[level, kind, :, cols] = (
                        centre + jnp.where(lane_last, fresh[kind][1], left)
                        + jnp.where(lane_first, behind[kind], right))
                behind = [held[kind][2] for kind in range(species)]
            held = fresh
        return carry

    lax.fori_loop(0, levels, stencils, 0)

    used = (blocks + 2 * per_row) * species
    spare = jnp.zeros((own_terms.shape[0] - used, inv_cells), F32)
    own_terms[used:, :] = spare
    their_terms[used:, :] = spare

    def term_copy(part):
        if part < per_row:
            span = pl.ds(part * rows * species, rows * species)
        else:
            span = pl.ds(blocks * species, per_row * SUB)
        return pltpu.make_async_remote_copy(
            src_ref=own_terms.at[span], dst_ref=their_terms.at[span],
            send_sem=send_a.at[part], recv_sem=recv_a.at[part],
            device_id=partner, device_id_type=MESH)

    def solve(c, kind):
        cols = column(c)
        below, held = None, []
        for level in range(levels):
            value = solved[level, kind, :, cols] * inverse_v[level, :, cols]
            if level > 0:
                value = value + carry_v[level, :, cols] * below
            below = value
            held.append(value)
        for level in range(levels - 1, -1, -1):
            value = held[level]
            if level < levels - 1:
                value = value - upper_v[level + 1, :, cols] * below
            solved[level, kind, :, cols] = value
            below = value
        flat[c, pl.ds(kind, rows, stride=species), :] = below

    def units(part):
        spans = range(part * lane_parts, (part + 1) * lane_parts)
        return [(c, kind) for c in spans for kind in range(species)] if part < per_row else []

    def regridded(surface, weights):
        product = jnp.dot(surface.astype(BF16), jnp.concatenate(weights, axis=1), preferred_element_type=F32)
        value = product[:, :inv_cells]
        for j in range(1, len(weights)):
            value = jnp.where(edge_ids >= j * species, product[:, j * inv_cells:(j + 1) * inv_cells], value)
        return value

    for unit in units(0):
        solve(*unit)
    for part in range(per_row):
        regrid_copy(part).wait()
        ahead_units, pairs = units(part + 1), rows // group
        for pair in range(pairs):
            for unit in ahead_units[pair::pairs]:
                solve(*unit)
            lines = slice(pair * SUB, (pair + 1) * SUB)
            surface = jnp.concatenate(
                [flat[part * lane_parts + p, lines, :] for p in range(lane_parts)], axis=1)
            weights = [regrid_v[pair * group + j, part] for j in range(group)]
            start = part * rows * species + pair * SUB
            own_terms[start:start + SUB, :] = regridded(surface, weights)
        term_copy(part).start()

    send_ids.wait_recv()
    unit = faces * NI
    height = chips * unit
    place = lax.broadcasted_iota(jnp.int32, (height, half_k), 0)
    to_chip = chip + place // unit
    to_chip = jnp.where(to_chip >= chips, to_chip - chips, to_chip)
    spot_of = lax.rem(place, unit) // NI
    to_face = jnp.full((height, half_k), face, jnp.int32)
    for spot in range(1, faces):
        to_face = jnp.where(spot_of == spot, face_of[spot], to_face)
    target = ((to_face * tiles + 2 * to_chip + core) * NI + lax.rem(place, NI)).astype(F32)
    select = jnp.concatenate(
        [(jnp.broadcast_to(ref[0:1, :], (height, half_k)) == target).astype(F32) for ref in (own_ids, their_ids)],
        axis=1).astype(BF16)
    small_first, small_last = lane_first[:SUB], lane_last[:SUB]
    nothing = jnp.zeros((SUB, LANES), F32)

    def edge_forward(part):
        for copy in edge_copies(part):
            copy.wait_recv()
        for j in range(group):
            level = part * group + j
            held, behind = None, nothing
            for c in range(chunks + 1):
                fresh = (None, nothing, nothing)
                if c < chunks:
                    cols = column(c)
                    south, north = edge_rates[0, level, :, cols], edge_rates[1, level, :, cols]
                    west, east = from_west[part, :, cols], from_east[part, :, cols]
                    if j > 0:
                        west = pltpu.roll(west, SUB - j * species, 0)
                    if j < group - 1:
                        east = pltpu.roll(east, SUB - (j + 1) * species, 0)
                    moved = jnp.where(upper_half, west, east)
                    fresh = ((1.0 - south - north) * moved,
                             pltpu.roll(south * moved, LANES - 1, 1), pltpu.roll(north * moved, 1, 1))
                if c > 0:
                    cols = column(c - 1)
                    centre, left, right = held
                    value = centre + jnp.where(small_last, fresh[1], left) + jnp.where(small_first, behind, right)
                    value = value * edge_rates[2, level, :, cols]
                    if level > 0:
                        value = value + edge_rates[3, level, :, cols] * edge[level - 1, :, cols]
                    edge[level, :, cols] = value
                    behind = right
                held = fresh

    for part in range(groups):
        edge_forward(part)
    odd = lax.rem(final_rows, group) == 1
    lone = jnp.logical_and(upper_half, final_rows == 0)
    surfaces = []
    for c in range(chunks):
        cols = column(c)
        below = edge[levels - 1, :, cols]
        for level in range(levels - 2, -1, -1):
            below = edge[level, :, cols] - edge_rates[4, level, :, cols] * below
            edge[level, :, cols] = below
        slab = flat[c, 0:SUB, :]
        for pair in range(1, rows // group):
            slab = jnp.where(final_rows >= pair * group, flat[c, pair * SUB:(pair + 1) * SUB, :], slab)
        slab = jnp.where(odd, slab, pltpu.roll(slab, species, 0))
        below = below + jnp.where(lone, pltpu.roll(below, species, 0), 0.0)
        surfaces.append(below + jnp.where(upper_half, flat[c, 0:SUB, :], slab))
    for part in range(per_row):
        surface = jnp.concatenate(surfaces[part * lane_parts:(part + 1) * lane_parts], axis=1)
        start = blocks * species + part * SUB
        own_terms[start:start + SUB, :] = regridded(surface, [regrid_v[0, part], regrid_v[final_row, part]])
    term_copy(per_row).start()

    for part in range(per_row + 1):
        term_copy(part).wait_recv()
    values = jnp.concatenate(
        [jnp.concatenate([ref[pl.ds(kind, half_k, stride=species), :] for kind in range(species)], axis=1)
         for ref in (own_terms, their_terms)], axis=0)
    total = sum(jnp.dot(select, piece, preferred_element_type=F32) for piece in pieces(values, 2))
    for step in range(chips):
        for spot in range(faces):
            start = step * unit + spot * NI
            sums[step, spot] = total[start:start + NI]

    spots = list(range(1, faces)) + [0]
    second, third = {}, {}
    for spot in spots:
        for step in range(1, chips):
            second[step, spot] = pltpu.make_async_remote_copy(
                src_ref=sums.at[step, spot], dst_ref=in_b.at[step - 1, spot],
                send_sem=send_b.at[step - 1, spot], recv_sem=recv_b.at[step - 1, spot],
                device_id=(face, 2 * chip_of[step] + core), device_id_type=MESH)
            second[step, spot].start()

    def add_edges(level, carry):
        for c in range(chunks):
            cols = column(c)
            for kind in range(species):
                solved[level, kind, :, cols] = (
                    solved[level, kind, :, cols] + jnp.where(first, edge[level, kind:kind + 1, cols], 0.0)
                    + jnp.where(last, edge[level, species + kind:species + kind + 1, cols], 0.0))
        return carry

    lax.fori_loop(0, levels, add_edges, 0)
    result = None
    for spot in spots:
        result = sums[0, spot]
        for step in range(1, chips):
            second[step, spot].wait_recv()
            result = result + in_b[step - 1, spot]
        if spot > 0:
            sum_c[spot - 1] = result
            third[spot] = pltpu.make_async_remote_copy(
                src_ref=sum_c.at[spot - 1], dst_ref=in_c.at[face],
                send_sem=send_c.at[spot - 1], recv_sem=recv_c.at[face],
                device_id=(face_of[spot], tile), device_id_type=MESH)
            third[spot].start()
    send_ids.wait_send()
    for part in range(groups):
        for copy in edge_copies(part):
            copy.wait_send()
    for part in range(per_row + 1):
        term_copy(part).wait_send()
    for copy in second.values():
        copy.wait_send()
    for spot in range(1, faces):
        pltpu.make_async_remote_copy(
            src_ref=sum_c.at[spot - 1], dst_ref=in_c.at[face_of[spot]],
            send_sem=send_c.at[spot - 1], recv_sem=recv_c.at[face_of[spot]],
            device_id=(face_of[spot], tile), device_id_type=MESH).wait_recv()
        result = result + in_c[face_of[spot]]
    for kind in range(species):
        grad_ref[:, kind, :] = result[:, kind * inv_cells:(kind + 1) * inv_cells]
    for copy in third.values():
        copy.wait_send()


def write_kernel(solved, grad, solved_out, grad_out, level_sem, grad_sem):
    copies = [pltpu.make_async_copy(grad, grad_out, grad_sem)]
    copies += [
        pltpu.make_async_copy(solved.at[level], solved_out.at[level], level_sem.at[level])
        for level in range(solved.shape[0])
    ]
    for copy in copies:
        copy.start()
    for copy in copies:
        copy.wait()


def per_device(faces, tiles, sensitivity, west_weight, east_weight, south_weight, north_weight,
               mixing_rate, extents, rotation, regrid_weight, owner, inv_slot):
    levels, species, rows, width = sensitivity.shape
    blocks, cells, inv_cells = regrid_weight.shape
    chips = tiles // 2
    hbm = pl.BlockSpec(memory_space=pltpu.HBM)
    vmem = pl.BlockSpec(memory_space=pltpu.VMEM)
    dma = pltpu.SemaphoreType.DMA
    groups = levels * species // SUB
    per_row = width // cells
    half_k = -(-(blocks + 2 * per_row) // LANES) * LANES
    field, line = (levels, rows, width), (groups, SUB, width)
    more = (levels + 1, rows, width)
    scratch = [pltpu.VMEM(shape, F32) for shape in [sensitivity.shape] + [field] * 4 + [more]]
    regrid_weight = regrid_weight.reshape(rows, per_row, cells, inv_cells)
    scratch += [pltpu.VMEM(regrid_weight.shape, regrid_weight.dtype)]
    shapes = [field, field, more] + [line] * 4 + [(5, levels, SUB, width), (levels, SUB, width)]
    shapes += [(width // LANES, rows * species, LANES)] + [(half_k * species, inv_cells)] * 2
    shapes += [(SUB, half_k)] * 2
    unit = (NI, species * inv_cells)
    shapes += [(chips, faces) + unit, (chips - 1, faces) + unit, (faces - 1,) + unit, (faces,) + unit]
    scratch += [pltpu.VMEM(shape, F32) for shape in shapes]
    scratch += [pltpu.SMEM(extents.shape, jnp.int32)] * 2 + [pltpu.VMEM((1, blocks), jnp.int32)] * 2
    scratch += [dma((4,)), dma((5, levels)), dma, dma((per_row,))]
    scratch += [dma((groups,))] * 4 + [dma((2,))] + [dma((per_row + 1,))] * 2
    scratch += [dma((chips - 1, faces))] * 2 + [dma((faces - 1,)), dma((faces,))]
    pin = functools.partial(pltpu.with_memory_space_constraint, memory_space=pltpu.HBM)
    operands = (extents, rotation, sensitivity, west_weight, east_weight, south_weight, north_weight,
                mixing_rate, regrid_weight, owner.reshape(1, blocks), inv_slot.reshape(1, blocks))
    outs = (
        jax.ShapeDtypeStruct(sensitivity.shape, F32),
        jax.ShapeDtypeStruct((NI, species, inv_cells), F32),
    )
    solved, grad = pl.pallas_call(
        functools.partial(step_kernel, faces, tiles),
        out_shape=outs,
        in_specs=[hbm] * 11,
        out_specs=(vmem, vmem),
        scratch_shapes=scratch,
        compiler_params=pltpu.CompilerParams(
            collective_id=0, has_side_effects=True, vmem_limit_bytes=44 << 20),
        name="step",
    )(*[pin(operand) for operand in operands])
    return pl.pallas_call(
        write_kernel,
        out_shape=outs,
        in_specs=[vmem, vmem],
        out_specs=(hbm, hbm),
        scratch_shapes=[dma((levels,)), dma],
        compiler_params=pltpu.CompilerParams(vmem_limit_bytes=8 << 20),
        name="write",
    )(solved, grad)


def solution(mesh):
    faces, tiles = mesh.shape["face"], mesh.shape["tile"]
    both = ("face", "tile")
    placed = (P(None, None, both, None),) + (P(None, both, None),) * 5 + (P(), P()) + (
        P(both, None, None), P(both, None), P(both))
    return jax.shard_map(
        functools.partial(per_device, faces, tiles),
        mesh=mesh,
        in_specs=placed,
        out_specs=(P(None, None, both, None), P(both, None, None)),
        check_vma=False,
    )
```
